512 devices in a mesh: pencil: 32 (over z, core), gz: 4 (over x), coarse: 4 (over y).
Axes of the slice: x: 4, y: 4, z: 16, core: 2. Of those that a mesh axis runs over, the one named last changes fastest.
Arguments:
- right_side: float32 [256, 64, 1024], P('pencil', 'coarse', 'gz'), may hold values from -6 to 6
- conductivity: float32 [256, 64, 1024], P('pencil', 'coarse', 'gz'), may hold values from 0.2 to 5
- guess: float32 [256, 64, 1024], P('pencil', 'coarse', 'gz'), may hold values from -4 to 4
Outputs:
- updated: float32 [256, 64, 1024], P('pencil', 'coarse', 'gz')
- smoothed_residual: float32 [256, 64, 1024], P('pencil', 'coarse', 'gz')
The draws below stay inside these ranges and needn't reach their ends.
All inputs are finite; a program needn't handle non-finite values.
Results may differ from the reference program's by a relative error of at most 0.00002.
Values sent between devices are 32-bit elements; how exact they have to be, the bound alone decides.
No kernel may reach another device: no remote copies, remote signals or barrier semaphores. Data moves between devices by JAX's collectives and lax.ppermute only.
A program may use at most 64 MiB of HBM per device.

```python
import math
import jax
import jax.numpy as jnp

KSWEEP = 4
NX = 256
NY = 64
NZ = 1024


def block_levels(rng, dims, pieces, smallest, top_value):
    factor_of = 1.0
    for axis_at, blocks in pieces:
        heights = jax.random.uniform(jax.random.fold_in(jax.random.fold_in(rng, 6), axis_at), (blocks,), jnp.float32, smallest / len(pieces), top_value / len(pieces))
        factor_of = factor_of * jnp.repeat(jnp.exp(heights), dims[axis_at] // blocks).reshape((-1,) + (1,) * (len(dims) - 1 - axis_at))
    return factor_of


def noise(key, shape, deviation, most, split=(), dtype=jnp.bfloat16):
    level = block_levels(key, shape, split, -0.22, 0.18) if split else 1.0
    drawn = jax.random.normal(key, shape, jnp.float32) * deviation * level
    return jnp.minimum(jnp.maximum(drawn, -most), most).astype(dtype)


def setup_inputs(seed: int = 0) -> dict:
    seeds = jax.random.split(jax.random.key(seed), 4)
    right_side = noise(seeds[0], (NX, NY, NZ), 1.0, 6.0, ((0, 32), (1, 4), (2, 4)), jnp.float32)
    conductivity = jnp.clip(jnp.exp(math.log(5.0) - 3.218876 * jax.random.uniform(seeds[1], (NX, NY, NZ), jnp.float32) ** block_levels(seeds[1], (NX, NY, NZ), ((0, 32), (1, 4), (2, 4)), -0.2, 0.2)), 0.2, 5.0)
    guess = noise(seeds[2], (NX, NY, NZ), 0.3, 4.0, ((0, 32), (1, 4), (2, 4)), jnp.float32)
    return {"right_side": right_side, "conductivity": conductivity, "guess": guess}


def face_terms(padded_k, scale):
    k = padded_k[1:-1, 1:-1, 1:-1]
    return [scale * 0.5 * (k + padded_k[:-2, 1:-1, 1:-1]), scale * 0.5 * (k + padded_k[2:, 1:-1, 1:-1]),
            scale * 0.5 * (k + padded_k[1:-1, :-2, 1:-1]), scale * 0.5 * (k + padded_k[1:-1, 2:, 1:-1]),
            scale * 0.5 * (k + padded_k[1:-1, 1:-1, :-2]), scale * 0.5 * (k + padded_k[1:-1, 1:-1, 2:])]


def diagonal_of(terms):
    return terms[0] + terms[1] + terms[2] + terms[3] + terms[4] + terms[5]


def operate(padded_v, terms, diag):
    v = padded_v[1:-1, 1:-1, 1:-1]
    out = diag * v - terms[0] * padded_v[:-2, 1:-1, 1:-1] - terms[1] * padded_v[2:, 1:-1, 1:-1]
    out = out - terms[2] * padded_v[1:-1, :-2, 1:-1] - terms[3] * padded_v[1:-1, 2:, 1:-1]
    return out - terms[4] * padded_v[1:-1, 1:-1, :-2] - terms[5] * padded_v[1:-1, 1:-1, 2:]


def restrict(field):
    a, b, c = field.shape
    return field.reshape(a // 2, 2, b // 2, 2, c // 2, 2).mean(axis=(1, 3, 5))


def reference(right_side, conductivity, guess):
    theta = 1.1
    delta = 0.8
    sigma = theta / delta
    rho0 = 1.0 / sigma
    rho1 = 1.0 / (2.0 * sigma - rho0)
    terms = face_terms(jnp.pad(conductivity, 1), 1.0)
    dfine = diagonal_of(terms)
    r0 = right_side - operate(jnp.pad(guess, 1), terms, dfine)
    d0 = r0 / (theta * dfine)
    r1 = r0 - operate(jnp.pad(d0, 1), terms, dfine)
    d1 = rho1 * rho0 * d0 + (2.0 * rho1 / delta) * r1 / dfine
    smoothed = r1 - operate(jnp.pad(d1, 1), terms, dfine)
    coarse_r = restrict(r0)
    coarse_k = restrict(conductivity)
    cterms = face_terms(jnp.pad(coarse_k, 1), 0.25)
    dcoarse = diagonal_of(cterms)
    correction = 0.8 * coarse_r / dcoarse
    for sweep in range(KSWEEP - 1):
        correction = correction + 0.8 * (coarse_r - operate(jnp.pad(correction, 1), cterms, dcoarse)) / dcoarse
    lifted = jnp.repeat(jnp.repeat(jnp.repeat(correction, 2, axis=0), 2, axis=1), 2, axis=2)
    updated = guess + d0 + d1 + lifted
    return updated, smoothed
```

```python
import functools

import jax
import jax.numpy as jnp
from jax import lax
from jax.experimental import pallas as pl
from jax.experimental.pallas import tpu as pltpu
from jax.sharding import PartitionSpec as P

KSWEEP = 4
THETA = 1.1
DELTA = 0.8
SIGMA = THETA / DELTA
RHO0 = 1.0 / SIGMA
RHO1 = 1.0 / (2.0 * SIGMA - RHO0)

NX, NY, NZ = 8, 16, 256
H = 8
RE = NY + 2 * H
RF = NY + H
ZE = NZ + 128
CX, CY = NX // 2, NY // 2
CE = RE // 2
GROUPS = 3 * NX
f32 = jnp.float32


def up(v, axis, by=1):
    return pltpu.roll(v, v.shape[axis] - by, axis)


def down(v, axis, by=1):
    return pltpu.roll(v, by, axis)


def lanes(shape):
    return lax.broadcasted_iota(jnp.int32, shape, len(shape) - 1)


def pack_kernel(where_ref, u_ref, k_ref, f_ref, up_ref, down_ref, z_ref):
    gz, cy = where_ref[0], where_ref[1]
    fields = (u_ref, k_ref, f_ref)
    for i, field in enumerate(fields):
        for p in range(NX):
            up_ref[i * NX + p] = field[p, NY - H :, :]
            down_ref[i * NX + p] = field[p, :H, :]
    group = lanes((NY, 128)) // H
    ends = []
    for first, start in ((NZ - 128, H), (0, 0)):
        tiles = []
        for t in range(2):
            tile = jnp.zeros((NY, 128), f32)
            for q in range(16):
                g = t * 16 + q
                if g < GROUPS:
                    cells = fields[g // NX][g % NX, :, first : first + 128]
                    shift = (H * q + start) % 128
                    moved = pltpu.roll(cells, shift, 1) if shift else cells
                    tile = jnp.where(group == q, moved, tile)
            tiles.append(tile)
        ends.append(jnp.concatenate(tiles, axis=1))
    z_ref[...] = jnp.zeros(z_ref.shape, f32)
    for end, to_z in zip(ends, (1, 3)):
        z = lax.rem(gz + to_z, 4) * 4
        z_ref[z + cy] = end
        z_ref[z + lax.rem(cy + 1, 4), :H] = end[NY - H :]
        z_ref[z + lax.rem(cy + 3, 4), :H] = end[:H]


def restrict_plane(plane, scratch_ref, even):
    pairs = plane + jnp.where(even, up(plane, 1), down(plane, 1))
    cols = []
    for t in range(ZE // 128):
        scratch_ref[t] = pairs[:, t * 128 : (t + 1) * 128]
        tile = scratch_ref.at[t]
        cols.append(tile[pl.ds(0, CE, stride=2), :] + tile[pl.ds(1, CE, stride=2), :])
    return 0.125 * jnp.concatenate(cols, axis=1)


def inner_rows(plane):
    row = lax.broadcasted_iota(jnp.int32, (H, ZE), 0)
    return jnp.concatenate(
        [plane[:NY], jnp.where(row < H // 2, plane[NY : NY + H], plane[NY + H :])], axis=0
    )


X_U, X_K, X_KI, X_R, X_C = 0, RE, 2 * RE, 2 * RE + 2 * RF, 2 * RE + 4 * RF
X_ROWS = X_C + 4 * CE


def block_kernel(
    where_ref, u_ref, k_ref, f_ref, up_ref, down_ref, z_ref,
    uo_ref, ko_ref, k_in_ref, r_in_ref, rc_ref, kc_ref, chip_ref, link_ref,
    ue_ref, ke_ref, fe_ref, tmp_ref,
):
    gz, cy, core = where_ref[0], where_ref[1], where_ref[2]
    lane = lanes((RE, 128))
    sides = []
    for from_z, inside in ((3, gz > 0), (1, gz < 3)):
        z = lax.rem(gz + from_z, 4) * 4
        rows = [
            z_ref[z + cy],
            jnp.where(cy < 3, z_ref[z + lax.rem(cy + 1, 4), :H], 0.0),
            jnp.where(cy > 0, z_ref[z + lax.rem(cy + 3, 4), :H], 0.0),
        ]
        sides.append(jnp.where(inside, jnp.concatenate(rows, axis=0), 0.0))
    for i, (own, ext) in enumerate(((u_ref, ue_ref), (k_ref, ke_ref), (f_ref, fe_ref))):
        for p in range(NX):
            g = i * NX + p
            t, q = divmod(g, 16)
            at = slice(t * 128, t * 128 + 128)
            before = pltpu.roll(sides[0][:, at], (120 - H * q) % 128, 1) if (120 - H * q) % 128 else sides[0][:, at]
            after = pltpu.roll(sides[1][:, at], (128 - H * q) % 128, 1) if q else sides[1][:, at]
            ext[p, :NY, :NZ] = own[p]
            ext[p, NY : NY + H, :NZ] = down_ref[g]
            ext[p, NY + H :, :NZ] = up_ref[g]
            ext[p, :, NZ:] = jnp.where(lane < H, after, jnp.where(lane >= 120, before, 0.0))
    even = lanes((RE, ZE)) % 2 == 0
    flux_x = None
    r_pair = k_pair = None
    for p in range(NX):
        k, u = ke_ref[p], ue_ref[p]
        flux = 0.5 * (k + up(k, 1)) * (u - up(u, 1))
        out = flux - down(flux, 1)
        flux = 0.5 * (k + up(k, 0)) * (u - up(u, 0))
        out = out + (flux - down(flux, 0))
        if flux_x is not None:
            out = out - flux_x
        if p < NX - 1:
            flux_x = 0.5 * (k + ke_ref[p + 1]) * (u - ue_ref[p + 1])
            out = out + flux_x
        r = fe_ref[p] - out
        r_in_ref[p] = inner_rows(r)
        k_in_ref[p] = inner_rows(k)
        if p % 2 == 0:
            r_pair, k_pair = r, k
        else:
            rc_ref[p // 2] = restrict_plane(r_pair + r, tmp_ref, even)
            kc_ref[p // 2] = restrict_plane(k_pair + k, tmp_ref, even)
    uo_ref[0], uo_ref[1] = ue_ref[0], ue_ref[NX - 1]
    ko_ref[0], ko_ref[1] = ke_ref[0], ke_ref[NX - 1]
    even_c = lanes((CE, ZE)) % 2 == 0
    for ref, last in ((chip_ref, core == 0), (link_ref, core == 1)):
        end = last.astype(jnp.int32)
        at, step = end * (NX - 1), 1 - 2 * end
        ref[X_U : X_U + RE] = ue_ref[at]
        ref[X_K : X_K + RE] = ke_ref[at]
        for d in range(2):
            ref[X_KI + d * RF : X_KI + (d + 1) * RF] = k_in_ref[at + (d + 1) * step]
            ref[X_R + d * RF : X_R + (d + 1) * RF] = r_in_ref[at + d * step]
        for d in range(CX):
            c = end * (CX - 1) + d * step
            ref[X_C + d * CE : X_C + (d + 1) * CE] = jnp.where(even_c, rc_ref[c], kc_ref[c])


def apply_faces(v, kx0, kx1, ky, kz, before, after, by=1):
    flux = kz * (v - up(v, 1, by))
    out = flux - down(flux, 1, by)
    flux = ky * (v - up(v, 0))
    out = out + (flux - down(flux, 0))
    return out + kx0 * (v - before) + kx1 * (v - after)


def final_kernel(
    where_ref, guess_ref, uo_ref, ko_ref, k_in_ref, r_in_ref, rc_ref, kc_ref, chip_ref, link_ref,
    new_ref, smooth_ref,
    k_ref, r_ref, inv_ref, d0_ref, d1_ref, ky_ref, kz_ref,
    q_ref, s_ref, cinv_ref, ec_ref, ed_ref, cy_ref, cz_ref, tmp_ref, lift_ref,
):
    core = where_ref[2]
    even = lanes((RE, ZE)) % 2 == 0
    even_c = lanes((CE, ZE)) % 2 == 0
    KO, RO, QO = 3, 2, 4
    for p in range(NX):
        k_ref[KO + p] = k_in_ref[p]
        r_ref[RO + p] = r_in_ref[p]
    for c in range(CX):
        q_ref[QO + c] = kc_ref[c]
        s_ref[QO + c] = rc_ref[c]
    for ref, last in ((chip_ref, core == 0), (link_ref, core == 1)):
        end = last.astype(jnp.int32)
        at, step = end * (NX - 1), 2 * end - 1
        un, kn = ref[X_U : X_U + RE], ref[X_K : X_K + RE]
        flux = 0.5 * (ko_ref[end] + kn) * (uo_ref[end] - un)
        inner = inner_rows(flux)
        r_ref[RO + at] = r_ref[RO + at] - inner
        k_ref[KO + at + step] = inner_rows(kn)
        r_ref[RO + at + step] = ref[X_R : X_R + RF] + inner
        r_ref[RO + at + 2 * step] = ref[X_R + RF : X_R + 2 * RF]
        for d in range(2):
            k_ref[KO + at + (d + 2) * step] = ref[X_KI + d * RF : X_KI + (d + 1) * RF]
        coarse = restrict_plane(flux, tmp_ref, even)
        ct = end * (CX - 1)
        s_ref[QO + ct] = s_ref[QO + ct] - coarse
        for d in range(CX):
            both = ref[X_C + d * CE : X_C + (d + 1) * CE]
            rc = jnp.where(even_c, both, down(both, 1))
            if d == 0:
                rc = rc + coarse
            s_ref[QO + ct + (d + 1) * step] = rc
            q_ref[QO + ct + (d + 1) * step] = jnp.where(even_c, up(both, 1), both)

    for p in range(-2, NX + 2):
        k = k_ref[KO + p]
        kx0 = 0.5 * (k + k_ref[KO + p - 1])
        kx1 = 0.5 * (k + k_ref[KO + p + 1])
        ky = 0.5 * (k + up(k, 0))
        kz = 0.5 * (k + up(k, 1))
        diag = kx0 + kx1 + (ky + down(ky, 0)) + (kz + down(kz, 1))
        inside = k > 0.0
        inv = jnp.where(inside, 1.0 / jnp.where(inside, diag, 1.0), 0.0)
        ky_ref[RO + p], kz_ref[RO + p], inv_ref[RO + p] = ky, kz, inv
        d0_ref[RO + p] = r_ref[RO + p] * inv * (1.0 / THETA)
    for p in range(-1, NX + 1):
        at = RO + p
        k = k_ref[KO + p]
        d0 = d0_ref[at]
        r1 = r_ref[at] - apply_faces(
            d0, 0.5 * (k + k_ref[KO + p - 1]), 0.5 * (k + k_ref[KO + p + 1]),
            ky_ref[at], kz_ref[at], d0_ref[at - 1], d0_ref[at + 1],
        )
        r_ref[at] = r1
        d1_ref[at] = RHO1 * RHO0 * d0 + (2.0 * RHO1 / DELTA) * r1 * inv_ref[at]
    for p in range(NX):
        at = RO + p
        k = k_ref[KO + p]
        d1 = d1_ref[at]
        out = r_ref[at] - apply_faces(
            d1, 0.5 * (k + k_ref[KO + p - 1]), 0.5 * (k + k_ref[KO + p + 1]),
            ky_ref[at], kz_ref[at], d1_ref[at - 1], d1_ref[at + 1],
        )
        smooth_ref[p] = out[:NY, :NZ]

    for c in range(-3, CX + 3):
        at = QO + c
        k = q_ref[at]
        cy = 0.125 * (k + up(k, 0))
        cz = 0.125 * (k + up(k, 1, 2))
        diag = 0.125 * (k + q_ref[at - 1]) + 0.125 * (k + q_ref[at + 1])
        diag = diag + (cy + down(cy, 0)) + (cz + down(cz, 1, 2))
        inside = k > 0.0
        inv = jnp.where(inside, 0.8 / jnp.where(inside, diag, 1.0), 0.0)
        cy_ref[at], cz_ref[at], cinv_ref[at] = cy, cz, inv
        ec_ref[at] = s_ref[at] * inv
    now, then = ec_ref, ed_ref
    for sweep in range(KSWEEP - 1):
        wide = KSWEEP - 2 - sweep
        for c in range(-wide, CX + wide):
            at = QO + c
            k = q_ref[at]
            e = now[at]
            res = s_ref[at] - apply_faces(
                e, 0.125 * (k + q_ref[at - 1]), 0.125 * (k + q_ref[at + 1]),
                cy_ref[at], cz_ref[at], now[at - 1], now[at + 1], 2,
            )
            then[at] = e + cinv_ref[at] * res
        now, then = then, now
    for c in range(CX):
        e = now[QO + c][:CY, :NZ]
        cols = []
        for t in range(NZ // 128):
            part = e[:, t * 128 : (t + 1) * 128]
            tile = lift_ref.at[t]
            tile[pl.ds(0, CY, stride=2), :] = part
            tile[pl.ds(1, CY, stride=2), :] = part
            cols.append(tile[...])
        lifted = jnp.concatenate(cols, axis=1)
        for p in (2 * c, 2 * c + 1):
            step = d0_ref[RO + p][:NY, :NZ] + d1_ref[RO + p][:NY, :NZ]
            new_ref[p] = guess_ref[p] + step + lifted


def call(kernel, outs, n_in, scratch, name, bytes_accessed, flops):
    vmem = pl.BlockSpec(memory_space=pltpu.VMEM)
    return pl.pallas_call(
        kernel,
        out_shape=[jax.ShapeDtypeStruct(s, f32) for s in outs],
        in_specs=[pl.BlockSpec(memory_space=pltpu.SMEM)] + [vmem] * (n_in - 1),
        out_specs=[vmem] * len(outs),
        scratch_shapes=[pltpu.VMEM(s, f32) for s in scratch],
        name=name,
        cost_estimate=pl.CostEstimate(flops=flops, bytes_accessed=bytes_accessed, transcendentals=0),
    )


def shifted(cells, axis, by):
    count = lax.axis_size(axis)
    return lax.ppermute(cells, axis, [(i, i + by) for i in range(count) if 0 <= i + by < count])


def swapped(cells, axis, first):
    count = lax.axis_size(axis)
    pairs = []
    for i in range(first, count - 1, 2):
        pairs += [(i, i + 1), (i + 1, i)]
    return lax.ppermute(cells, axis, pairs)


def on_device(right_side, conductivity, guess):
    where = jnp.stack(
        [lax.axis_index("gz"), lax.axis_index("coarse"), lax.axis_index("pencil") % 2]
    ).astype(jnp.int32)
    fields = (guess, conductivity, right_side)
    upward, downward, ends = call(
        pack_kernel,
        [(GROUPS, H, NZ), (GROUPS, H, NZ), (16, NY, 256)],
        4, [], "pack", 1 << 20, 1 << 18,
    )(where, *fields)
    ends = lax.all_to_all(ends, ("gz", "coarse"), 0, 0)
    upward = shifted(upward, "coarse", 1)
    downward = shifted(downward, "coarse", -1)
    kept = call(
        block_kernel,
        [
            (2, RE, ZE), (2, RE, ZE), (NX, RF, ZE), (NX, RF, ZE), (CX, CE, ZE), (CX, CE, ZE),
            (X_ROWS, ZE), (X_ROWS, ZE),
        ],
        7, [(NX, RE, ZE)] * 3 + [(ZE // 128, RE, 128)], "block", 3 << 20, 1 << 22,
    )(where, *fields, upward, downward, ends)
    chip = swapped(kept[6], "pencil", 0)
    link = swapped(kept[7], "pencil", 1)
    fine, wide = (NX + 4, RF, ZE), (NX + 6, RF, ZE)
    coarse = (CX + 8, CE, ZE)
    return tuple(
        call(
            final_kernel,
            [(NX, NY, NZ), (NX, NY, NZ)],
            10,
            [wide] + [fine] * 6 + [coarse] * 7 + [(ZE // 128, RE, 128), (NZ // 128, NY, 128)],
            "final", 4 << 20, 1 << 23,
        )(where, guess, *kept[:6], chip, link)
    )


def solution(mesh):
    spec = P("pencil", "coarse", "gz")
    return jax.shard_map(
        on_device,
        mesh=mesh,
        in_specs=(spec, spec, spec),
        out_specs=(spec, spec),
        check_vma=False,
    )
```

```python
import jax
import jax.numpy as jnp
from jax import lax
from jax.experimental import pallas as pl
from jax.experimental.pallas import tpu as pltpu
from jax.sharding import PartitionSpec as P


THETA = 1.1
DELTA = 0.8
SIGMA = THETA / DELTA
RHO0 = 1.0 / SIGMA
RHO1 = 1.0 / (2.0 * SIGMA - RHO0)

NX, NY, NZ = 8, 16, 256
H = 8
RE = NY + 2 * H
RF = NY + H
ZE = NZ + 128
CX, CY = NX // 2, NY // 2
CE = RE // 2
GROUPS = 3 * NX
f32 = jnp.float32


def up(v, axis, by=1):
    return pltpu.roll(v, v.shape[axis] - by, axis)


def down(v, axis, by=1):
    return pltpu.roll(v, by, axis)


def lanes(shape):
    return lax.broadcasted_iota(jnp.int32, shape, len(shape) - 1)


def pack_kernel(
    u_hbm, k_hbm, f_hbm,
    u_ref, k_ref, f_ref, up_ref, down_ref, z_hbm,
    end_ref, own_sem, end_sem,
):
    gz, cy = lax.axis_index("gz"), lax.axis_index("coarse")
    fields = (u_ref, k_ref, f_ref)
    copies = []
    for i, (far, near) in enumerate(zip((u_hbm, k_hbm, f_hbm), fields)):
        for half in range(2):
            at = pl.ds(half * NX // 2, NX // 2)
            copies.append(pltpu.make_async_copy(far.at[at], near.at[at], own_sem.at[2 * i + half]))
            copies[-1].start()
    for copy in copies:
        copy.wait()
    group = lanes((NY, 128)) // H
    sends = []
    for side, (first, start, to_z) in enumerate(((NZ - 128, H, 1), (0, 0, 3))):
        for t in range(2):
            tile = jnp.zeros((NY, 128), f32)
            for q in range(16):
                g = t * 16 + q
                if g < GROUPS:
                    cells = fields[g // NX][g % NX, :, first : first + 128]
                    shift = (H * q + start) % 128
                    moved = pltpu.roll(cells, shift, 1) if shift else cells
                    tile = jnp.where(group == q, moved, tile)
            end_ref[side, :, t * 128 : (t + 1) * 128] = tile
        z = lax.rem(gz + to_z, 4) * 4
        end = end_ref.at[side]
        for j, (src, dst) in enumerate((
            (end, z_hbm.at[z + cy]),
            (end.at[pl.ds(NY - H, H)], z_hbm.at[z + lax.rem(cy + 1, 4), pl.ds(0, H)]),
            (end.at[pl.ds(0, H)], z_hbm.at[z + lax.rem(cy + 3, 4), pl.ds(0, H)]),
        )):
            sends.append(pltpu.make_async_copy(src, dst, end_sem.at[3 * side + j]))
            sends[-1].start()
    for i, field in enumerate(fields):
        for p in range(NX):
            up_ref[i * NX + p] = field[p, NY - H :, :]
            down_ref[i * NX + p] = field[p, :H, :]
    for copy in sends:
        copy.wait()


def restrict_plane(plane, scratch_ref, even, scale):
    pairs = plane + jnp.where(even, up(plane, 1), down(plane, 1))
    cols = []
    for t in range(ZE // 128):
        scratch_ref[t] = pairs[:, t * 128 : (t + 1) * 128]
        tile = scratch_ref.at[t]
        cols.append(tile[pl.ds(0, CE, stride=2), :] + tile[pl.ds(1, CE, stride=2), :])
    return scale * jnp.concatenate(cols, axis=1)


def place(core, p, count):
    return core * (count - 1) + (1 - 2 * core) * p


def inner_rows(plane):
    row = lax.broadcasted_iota(jnp.int32, (H, ZE), 0)
    return jnp.concatenate(
        [plane[:NY], jnp.where(row < H // 2, plane[NY : NY + H], plane[NY + H :])], axis=0
    )


X_U, X_K, X_K2, X_K3, X_R1, X_R2, X_C = 0, 4, 8, 11, 13, 16, 18
X_GROUPS = X_C + 3 * 2 + 1
X_TAIL = X_GROUPS


def send_rows(ref, tails, first, plane):
    for j in range(plane.shape[0] // 8):
        rows = plane[j * 8 : (j + 1) * 8]
        ref[first + j] = rows[:, :NZ]
        tails[first + j] = rows[:, NZ:]


def send_tails(ref, tails):
    lane = lanes((8, 128)) // 16
    for half in range(4):
        tile = jnp.zeros((8, 128), f32)
        for j in range(8):
            g = half * 8 + j
            if g < X_GROUPS:
                shift = (16 * j + 8) % 128
                tile = jnp.where(lane == j, pltpu.roll(tails[g], shift, 1), tile)
        ref[X_TAIL + half // 2, :, (half % 2) * 128 : (half % 2) * 128 + 128] = tile


def received_rows(ref, first, groups):
    rows = []
    for g in range(first, first + groups):
        half, j = divmod(g, 8)
        tile = ref[X_TAIL + half // 2, :, (half % 2) * 128 : (half % 2) * 128 + 128]
        rows.append(jnp.concatenate([ref[g], pltpu.roll(tile, (120 - 16 * j) % 128, 1)], axis=1) if (120 - 16 * j) % 128 else jnp.concatenate([ref[g], tile], axis=1))
    return jnp.concatenate(rows, axis=0)


def block_kernel(
    u_ref, k_ref, f_ref, up_ref, down_ref, z_ref,
    uo_ref, ko_ref, k_in_ref, r_in_ref, rc_ref, kc_ref, chip_ref, link_ref,
    ue_ref, ke_ref, fe_ref, tmp_ref,
):
    gz, cy, core = lax.axis_index("gz"), lax.axis_index("coarse"), lax.rem(lax.axis_index("pencil"), 2)
    lane = lanes((RE, 128))
    sides = []
    for from_z, inside in ((3, gz > 0), (1, gz < 3)):
        z = lax.rem(gz + from_z, 4) * 4
        rows = [
            z_ref[z + cy],
            jnp.where(cy < 3, z_ref[z + lax.rem(cy + 1, 4), :H], 0.0),
            jnp.where(cy > 0, z_ref[z + lax.rem(cy + 3, 4), :H], 0.0),
        ]
        sides.append(jnp.where(inside, jnp.concatenate(rows, axis=0), 0.0))
    for i, (own, ext) in enumerate(((u_ref, ue_ref), (k_ref, ke_ref), (f_ref, fe_ref))):
        scale = (lambda v: 0.5 * v) if i == 1 else (lambda v: v)
        for p in range(NX):
            g = i * NX + p
            t, q = divmod(g, 16)
            before, after = (side[:, t * 128 : t * 128 + 128] for side in sides)
            if (120 - H * q) % 128:
                before = pltpu.roll(before, (120 - H * q) % 128, 1)
            if q:
                after = pltpu.roll(after, 128 - H * q, 1)
            ext[p, :NY, :NZ] = scale(own[p])
            ext[p, NY : NY + H, :NZ] = scale(down_ref[g])
            ext[p, NY + H :, :NZ] = scale(up_ref[g])
            ext[p, :, NZ:] = scale(jnp.where(lane < H, after, jnp.where(lane >= 120, before, 0.0)))
    even = lanes((RE, ZE)) % 2 == 0
    flux_x = None
    r_pair = k_pair = None
    for p in range(NX):
        k, u = ke_ref[p], ue_ref[p]
        flux = (k + up(k, 1)) * (u - up(u, 1))
        out = flux - down(flux, 1)
        flux = (k + up(k, 0)) * (u - up(u, 0))
        out = out + (flux - down(flux, 0))
        if flux_x is not None:
            out = out - flux_x
        if p < NX - 1:
            flux_x = (k + ke_ref[p + 1]) * (u - ue_ref[p + 1])
            out = out + flux_x
        r = fe_ref[p] - out
        q = place(core, p, NX)
        r_in_ref[q] = inner_rows(r)
        k_in_ref[q] = inner_rows(k)
        if p % 2 == 0:
            r_pair, k_pair = r, k
        else:
            c = place(core, p // 2, CX)
            rc_ref[c] = restrict_plane(r_pair + r, tmp_ref, even, 0.125)
            kc_ref[c] = restrict_plane(k_pair + k, tmp_ref, even, 0.03125)
    for i in range(2):
        end = place(core, i * (NX - 1), NX)
        uo_ref[i], ko_ref[i] = ue_ref[end], ke_ref[end]
    even_c = lanes((CE, ZE)) % 2 == 0
    for i, ref in enumerate((link_ref, chip_ref)):
        at, step, c = i * (NX - 1), 1 - 2 * i, i * (CX - 1)
        tails = {}
        send_rows(ref, tails, X_U, uo_ref[i])
        send_rows(ref, tails, X_K, ko_ref[i])
        send_rows(ref, tails, X_K2, k_in_ref[at + step])
        send_rows(ref, tails, X_K3, k_in_ref[at + 2 * step, :NY])
        send_rows(ref, tails, X_R1, r_in_ref[at])
        send_rows(ref, tails, X_R2, r_in_ref[at + step, :NY])
        for d in range(CX):
            both = jnp.where(even_c, rc_ref[c + d * step], kc_ref[c + d * step])
            send_rows(ref, tails, X_C + 2 * d, both if d < 3 else both[:CY])
        send_tails(ref, tails)


def faces_yz(k, by=1):
    ky, kz = k + up(k, 0), k + up(k, 1, by)
    return ky, kz, (ky + down(ky, 0)) + (kz + down(kz, 1, by))


def flux_yz(v, ky, kz, by=1):
    flux = kz * (v - up(v, 1, by))
    out = flux - down(flux, 1, by)
    flux = ky * (v - up(v, 0))
    return out + (flux - down(flux, 0))


def inverse(k, diag, scale=1.0):
    return jnp.where(k > 0.0, scale / diag, 0.0)


def step_d1(r1, d0, inv):
    return (RHO1 * RHO0) * d0 + (2.0 * RHO1 / DELTA) * (r1 * inv)


def main(v):
    return v[:NY, :NZ]


def open_message(msg, u_end, k_end, r_end, rc_end, tmp_ref):
    even, even_c = lanes((RE, ZE)) % 2 == 0, lanes((CE, ZE)) % 2 == 0
    none = jnp.zeros((RF - NY, ZE), f32)
    un, kn = received_rows(msg, X_U, 4), received_rows(msg, X_K, 4)
    flux = (k_end + kn) * (u_end - un)
    inner = inner_rows(flux)
    coarse = restrict_plane(flux, tmp_ref, even, 0.125)
    ks = [inner_rows(kn), received_rows(msg, X_K2, 3)]
    ks.append(jnp.concatenate([received_rows(msg, X_K3, 2), none], axis=0))
    rs = [received_rows(msg, X_R1, 3) + inner]
    rs.append(jnp.concatenate([received_rows(msg, X_R2, 2), none], axis=0))
    kcs, rcs = [], []
    for d in range(CX):
        if d < 3:
            both = received_rows(msg, X_C + 2 * d, 2)
            rc = jnp.where(even_c, both, down(both, 1))
            rcs.append(rc + coarse if d == 0 else rc)
        else:
            both = jnp.concatenate([received_rows(msg, X_C + 2 * d, 1), none], axis=0)
        kcs.append(jnp.where(even_c, up(both, 1), both))
    return r_end - inner, ks, rs, rc_end - coarse, kcs, rcs


def chip_kernel(
    u_ref, uo_ref, ko_ref, k_ref, r_ref, rc_ref, kc_ref, msg_ref,
    ky_ref, kz_ref, inv_ref, d0_ref, r1_ref, d1_ref, sum_ref, smooth_ref,
    q_ref, s_ref, cy_ref, cz_ref, cinv_ref, e0_ref, e1_ref, e2_ref,
    kx_ref, rx_ref, tmp_ref,
):
    core = lax.rem(lax.axis_index("pencil"), 2)
    r_end, ks, rs, rc_end, kcs, rcs = open_message(
        msg_ref, uo_ref[1], ko_ref[1], r_ref[NX - 1], rc_ref[CX - 1], tmp_ref
    )
    for d, k in enumerate(ks):
        kx_ref[d] = k
    for d, r in enumerate([r_end] + rs):
        rx_ref[d] = r
    for c in range(CX):
        q_ref[c], q_ref[CX + c] = kc_ref[c], kcs[c]
        s_ref[c] = rc_ref[c] if c < CX - 1 else rc_end
        if c < 3:
            s_ref[CX + c] = rcs[c]

    def k_at(p):
        return k_ref[p] if p < NX else kx_ref[p - NX]

    def r_at(p):
        return r_ref[p] if p < NX - 1 else rx_ref[p - NX + 1]

    kx = None
    for p in range(NX + 2):
        k = k_at(p)
        ky_ref[p], kz_ref[p], diag = faces_yz(k)
        before, kx = kx, k + k_at(p + 1)
        if p == 0:
            inv_ref[p] = diag + kx
        else:
            inv = inverse(k, diag + before + kx)
            inv_ref[p] = inv
            d0_ref[p] = r_at(p) * inv * (1.0 / THETA)
    flux_x = (k_at(1) + k_at(2)) * (d0_ref[1] - d0_ref[2])
    for p in range(2, NX + 1):
        d0 = d0_ref[p]
        out = flux_yz(d0, ky_ref[p], kz_ref[p]) - flux_x
        flux_x = (k_at(p) + k_at(p + 1)) * (d0 - d0_ref[p + 1])
        r1 = r_at(p) - (out + flux_x)
        d1 = step_d1(r1, d0, inv_ref[p])
        r1_ref[p], d1_ref[p] = r1, d1
        if p < NX:
            sum_ref[p] = u_ref[place(core, p, NX)] + main(d0) + main(d1)
    flux_x = main((k_at(2) + k_at(3)) * (d1_ref[2] - d1_ref[3]))
    for p in range(3, NX):
        d1 = d1_ref[p]
        out = main(flux_yz(d1, ky_ref[p], kz_ref[p])) - flux_x
        flux_x = main((k_at(p) + k_at(p + 1)) * (d1 - d1_ref[p + 1]))
        smooth_ref[p] = main(r1_ref[p]) - (out + flux_x)

    kx = None
    for c in range(CX + 3):
        k = q_ref[c]
        cy_ref[c], cz_ref[c], diag = faces_yz(k, 2)
        before, kx = kx, k + q_ref[c + 1]
        if c == 0:
            cinv_ref[c] = diag + kx
        else:
            inv = inverse(k, diag + before + kx, 0.8)
            cinv_ref[c] = inv
            e0_ref[c] = s_ref[c] * inv
    for now, then, first, last in ((e0_ref, e1_ref, 2, CX + 1), (e1_ref, e2_ref, 3, CX)):
        flux_x = (q_ref[first - 1] + q_ref[first]) * (now[first - 1] - now[first])
        for c in range(first, last + 1):
            e = now[c]
            out = flux_yz(e, cy_ref[c], cz_ref[c], 2) - flux_x
            flux_x = (q_ref[c] + q_ref[c + 1]) * (e - now[c + 1])
            then[c] = e + cinv_ref[c] * (s_ref[c] - (out + flux_x))


def final_kernel(
    u_ref, uo_ref, ko_ref, k_ref, r_ref,
    ky_ref, kz_ref, inv_ref, d0_ref, r1_ref, d1_ref, sum_ref, smooth_ref,
    q_ref, s_ref, cy_ref, cz_ref, cinv_ref, e0_ref, e1_ref, e2_ref, msg_ref,
    new_hbm, smooth_hbm,
    k_x, r_x, ky_x, kz_x, inv_x, d0_x, d1_x, q_x, s_x, cy_x, cz_x, cinv_x, e0_x, e1_x, e2_x,
    tmp_ref, lift_ref, new_ref, out_ref, new_sem, smooth_sem,
):
    core = lax.rem(lax.axis_index("pencil"), 2)
    copies = []

    def put(src, dst, sem, p):
        copies.append(pltpu.make_async_copy(src, dst.at[place(core, p, NX)], sem.at[p]))
        copies[-1].start()

    for p in range(3, NX):
        put(smooth_ref.at[p], smooth_hbm, smooth_sem, p)
    OFF, COFF = 3, 4
    r_end, ks, rs, rc_end, kcs, rcs = open_message(
        msg_ref, uo_ref[0], ko_ref[0], r_ref[0], s_ref[0], tmp_ref
    )
    for d, k in enumerate(ks):
        k_x[OFF - 1 - d] = k
    for d, r in enumerate([r_end] + rs):
        r_x[OFF - d] = r
    for d, k in enumerate(kcs):
        q_x[COFF - 1 - d] = k
    for d, r in enumerate([rc_end] + rcs):
        s_x[COFF - d] = r

    def at(near, own, p, first=0, off=OFF):
        return own[p] if p >= first else near[off + p]

    def k_at(p):
        return at(k_x, k_ref, p)

    def d0_at(p):
        return at(d0_x, d0_ref, p, 1)

    def d1_at(p):
        return at(d1_x, d1_ref, p, 2)

    kx = k_at(-3) + k_at(-2)
    for p in range(-2, 1):
        k = k_at(p)
        before, kx = kx, k + k_at(p + 1)
        if p < 0:
            ky_x[OFF + p], kz_x[OFF + p], diag = faces_yz(k)
            diag = diag + before + kx
        else:
            diag = inv_ref[p] + before
        inv = inverse(k, diag)
        inv_x[OFF + p] = inv
        d0_x[OFF + p] = r_x[OFF + p] * inv * (1.0 / THETA)
    flux_x = (k_at(-2) + k_at(-1)) * (d0_at(-2) - d0_at(-1))
    for p in range(-1, 2):
        d0 = d0_at(p)
        out = flux_yz(d0, at(ky_x, ky_ref, p), at(kz_x, kz_ref, p)) - flux_x
        flux_x = (k_at(p) + k_at(p + 1)) * (d0 - d0_at(p + 1))
        r1 = at(r_x, r_ref, p, 1) - (out + flux_x)
        r_x[OFF + p] = r1
        d1_x[OFF + p] = step_d1(r1, d0, at(inv_x, inv_ref, p, 1))
    flux_x = main((k_at(-1) + k_at(0)) * (d1_at(-1) - d1_at(0)))
    for p in range(3):
        d1 = d1_at(p)
        out = main(flux_yz(d1, ky_ref[p], kz_ref[p])) - flux_x
        flux_x = main((k_at(p) + k_at(p + 1)) * (d1 - d1_at(p + 1)))
        out_ref[p] = main(at(r_x, r1_ref, p, 2)) - (out + flux_x)
        put(out_ref.at[p], smooth_hbm, smooth_sem, p)

    def q_at(c):
        return at(q_x, q_ref, c, 0, COFF)

    kx = q_at(-4) + q_at(-3)
    for c in range(-3, 1):
        k = q_at(c)
        before, kx = kx, k + q_at(c + 1)
        if c < 0:
            cy_x[COFF + c], cz_x[COFF + c], diag = faces_yz(k, 2)
            diag = diag + before + kx
        else:
            diag = cinv_ref[c] + before
        inv = inverse(k, diag, 0.8)
        cinv_x[COFF + c] = inv
        e0_x[COFF + c] = s_x[COFF + c] * inv
    for (near, own, known), store, first in (
        ((e0_x, e0_ref, 1), e1_x, -2), ((e1_x, e1_ref, 2), e2_x, -1), ((e2_x, e2_ref, 3), None, 0)
    ):
        def e_at(c):
            return at(near, own, c, known, COFF)

        flux_x = (q_at(first - 1) + q_at(first)) * (e_at(first - 1) - e_at(first))
        for c in range(first, first + 4):
            e = e_at(c)
            cy, cz = at(cy_x, cy_ref, c, 0, COFF), at(cz_x, cz_ref, c, 0, COFF)
            out = flux_yz(e, cy, cz, 2) - flux_x
            flux_x = (q_at(c) + q_at(c + 1)) * (e - e_at(c + 1))
            rest = at(s_x, s_ref, c, 1, COFF) - (out + flux_x)
            e = e + at(cinv_x, cinv_ref, c, 1, COFF) * rest
            if store is not None:
                store[COFF + c] = e
                continue
            cols = []
            for t in range(NZ // 128):
                part = e[:CY, t * 128 : (t + 1) * 128]
                tile = lift_ref.at[t]
                tile[pl.ds(0, CY, stride=2), :] = part
                tile[pl.ds(1, CY, stride=2), :] = part
                cols.append(tile[...])
            lifted = jnp.concatenate(cols, axis=1)
            for p in (2 * c, 2 * c + 1):
                if p < 2:
                    done = u_ref[place(core, p, NX)] + main(d0_at(p)) + main(d1_at(p))
                else:
                    done = sum_ref[p]
                new_ref[p] = done + lifted
                put(new_ref.at[p], new_hbm, new_sem, p)
    for copy in copies:
        copy.wait()


def call(kernel, outs, specs, scratch, bytes_accessed, flops):
    spaces = {"s": pltpu.SMEM, "v": pltpu.VMEM, "h": pltpu.HBM}
    return pl.pallas_call(
        kernel,
        out_shape=[jax.ShapeDtypeStruct(tuple(s), f32) for s in outs],
        in_specs=[pl.BlockSpec(memory_space=spaces[s]) for s in specs],
        out_specs=[
            pl.BlockSpec(memory_space=pl.ANY if isinstance(s, list) else pltpu.VMEM) for s in outs
        ],
        scratch_shapes=[pltpu.VMEM(s, f32) if isinstance(s, tuple) else s for s in scratch],
        compiler_params=pltpu.CompilerParams(vmem_limit_bytes=16 << 20),
        cost_estimate=pl.CostEstimate(flops=flops, bytes_accessed=bytes_accessed, transcendentals=0),
    )


def shifted(cells, axis, by):
    count = lax.axis_size(axis)
    return lax.ppermute(cells, axis, [(i, i + by) for i in range(count) if 0 <= i + by < count])


def swapped(cells, axis, first):
    count = lax.axis_size(axis)
    pairs = []
    for i in range(first, count - 1, 2):
        pairs += [(i, i + 1), (i + 1, i)]
    return lax.ppermute(cells, axis, pairs)


def on_device(right_side, conductivity, guess):
    own = (NX, NY, NZ)
    dma = pltpu.SemaphoreType.DMA
    u, k, f, upward, downward, ends = call(
        pack_kernel,
        [own, own, own, (GROUPS, H, NZ), (GROUPS, H, NZ), [16, NY, 256]],
        "hhh", [(2, NY, 256), dma((6,)), dma((6,))], 1 << 20, 1 << 18,
    )(*(pltpu.with_memory_space_constraint(a, pltpu.HBM) for a in (guess, conductivity, right_side)))
    upward = shifted(upward, "coarse", 1)
    downward = shifted(downward, "coarse", -1)
    ends = lax.all_to_all(ends, ("gz", "coarse"), 0, 0)

    def fine(n):
        return (n, RF, ZE)

    def coarse(n):
        return (n, CE, ZE)

    message = (X_GROUPS + 2, 8, NZ)
    uo, ko, k_in, r_in, rc, kc, chip, link = call(
        block_kernel,
        [(2, RE, ZE), (2, RE, ZE), fine(NX), fine(NX), coarse(CX), coarse(CX), message, message],
        "vvvvvv", [(NX, RE, ZE)] * 3 + [(ZE // 128, RE, 128)], 3 << 20, 1 << 22,
    )(u, k, f, upward, downward, ends)
    chip = swapped(chip, "pencil", 0)
    link = swapped(link, "pencil", 1)
    half = call(
        chip_kernel,
        [fine(NX + 2)] * 4 + [fine(NX + 1)] * 2 + [own, own]
        + [coarse(2 * CX)] + [coarse(CX + 3)] * 7,
        "vvvvvvvv", [fine(3), fine(3), (ZE // 128, RE, 128)], 4 << 20, 1 << 22,
    )(u, uo, ko, k_in, r_in, rc, kc, chip)
    return tuple(
        call(
            final_kernel, [list(own), list(own)], "v" * 22,
            [fine(3), fine(5)] + [fine(5)] * 5 + [coarse(4)] + [coarse(8)] * 7
            + [(ZE // 128, RE, 128), (NZ // 128, NY, 128), own, (3, NY, NZ), dma((NX,)), dma((NX,))],
            4 << 20, 1 << 22,
        )(u, uo, ko, k_in, r_in, *half, link)
    )


def solution(mesh):
    spec = P("pencil", "coarse", "gz")
    return jax.shard_map(
        on_device,
        mesh=mesh,
        in_specs=(spec, spec, spec),
        out_specs=(spec, spec),
        check_vma=False,
    )
```

```python
import jax
import jax.numpy as jnp
from jax import lax
from jax.experimental import pallas as pl
from jax.experimental.pallas import tpu as pltpu
from jax.sharding import PartitionSpec as P


THETA = 1.1
DELTA = 0.8
SIGMA = THETA / DELTA
RHO0 = 1.0 / SIGMA
RHO1 = 1.0 / (2.0 * SIGMA - RHO0)

NX, NY, NZ = 8, 16, 256
H = 8
RE = NY + 2 * H
RF = NY + H
ZE = NZ + 128
CX, CY = NX // 2, NY // 2
CE = RE // 2
GROUPS = 3 * NX
f32 = jnp.float32


def up(v, axis, by=1):
    return pltpu.roll(v, v.shape[axis] - by, axis)


def down(v, axis, by=1):
    return pltpu.roll(v, by, axis)


def lanes(shape):
    return lax.broadcasted_iota(jnp.int32, shape, len(shape) - 1)


def pack_kernel(
    u_hbm, k_hbm, f_hbm,
    u_ref, k_ref, f_ref, up_ref, down_ref, z_hbm,
    end_ref, own_sem, end_sem,
):
    gz, cy = lax.axis_index("gz"), lax.axis_index("coarse")
    fields = (u_ref, k_ref, f_ref)
    copies = []
    for i, (far, near) in enumerate(zip((u_hbm, k_hbm, f_hbm), fields)):
        for half in range(2):
            at = pl.ds(half * NX // 2, NX // 2)
            copies.append(pltpu.make_async_copy(far.at[at], near.at[at], own_sem.at[2 * i + half]))
            copies[-1].start()
    for copy in copies:
        copy.wait()
    group = lanes((NY, 128)) // H
    sends = []
    for side, (first, start, to_z) in enumerate(((NZ - 128, H, 1), (0, 0, 3))):
        for t in range(2):
            tile = jnp.zeros((NY, 128), f32)
            for q in range(16):
                g = t * 16 + q
                if g < GROUPS:
                    cells = fields[g // NX][g % NX, :, first : first + 128]
                    shift = (H * q + start) % 128
                    moved = pltpu.roll(cells, shift, 1) if shift else cells
                    tile = jnp.where(group == q, moved, tile)
            end_ref[side, :, t * 128 : (t + 1) * 128] = tile
        z = lax.rem(gz + to_z, 4) * 4
        end = end_ref.at[side]
        for j, (src, dst) in enumerate((
            (end, z_hbm.at[z + cy]),
            (end.at[pl.ds(NY - H, H)], z_hbm.at[z + lax.rem(cy + 1, 4), pl.ds(0, H)]),
            (end.at[pl.ds(0, H)], z_hbm.at[z + lax.rem(cy + 3, 4), pl.ds(0, H)]),
        )):
            sends.append(pltpu.make_async_copy(src, dst, end_sem.at[3 * side + j]))
            sends[-1].start()
    for i, field in enumerate(fields):
        for p in range(NX):
            up_ref[i * NX + p] = field[p, NY - H :, :]
            down_ref[i * NX + p] = field[p, :H, :]
    for copy in sends:
        copy.wait()


def restrict_plane(plane, scratch_ref, even, scale):
    pairs = plane + jnp.where(even, up(plane, 1), down(plane, 1))
    cols = []
    for t in range(ZE // 128):
        scratch_ref[t] = pairs[:, t * 128 : (t + 1) * 128]
        tile = scratch_ref.at[t]
        cols.append(tile[pl.ds(0, CE, stride=2), :] + tile[pl.ds(1, CE, stride=2), :])
    return scale * jnp.concatenate(cols, axis=1)


def place(core, p, count):
    return core * (count - 1) + (1 - 2 * core) * p


def inner_rows(plane):
    row = lax.broadcasted_iota(jnp.int32, (H, ZE), 0)
    return jnp.concatenate(
        [plane[:NY], jnp.where(row < H // 2, plane[NY : NY + H], plane[NY + H :])], axis=0
    )


X_U, X_K, X_K2, X_K3, X_R1, X_R2, X_C = 0, 4, 8, 11, 13, 16, 18
X_GROUPS = X_C + 3 * 2 + 1
X_TAIL = X_GROUPS


def send_rows(ref, tails, first, plane):
    for j in range(plane.shape[0] // 8):
        rows = plane[j * 8 : (j + 1) * 8]
        ref[first + j] = rows[:, :NZ]
        tails[first + j] = rows[:, NZ:]


def send_tails(ref, tails):
    lane = lanes((8, 128)) // 16
    for half in range(4):
        tile = jnp.zeros((8, 128), f32)
        for j in range(8):
            g = half * 8 + j
            if g < X_GROUPS:
                shift = (16 * j + 8) % 128
                tile = jnp.where(lane == j, pltpu.roll(tails[g], shift, 1), tile)
        ref[X_TAIL + half // 2, :, (half % 2) * 128 : (half % 2) * 128 + 128] = tile


def received_rows(ref, first, groups):
    rows = []
    for g in range(first, first + groups):
        half, j = divmod(g, 8)
        tile = ref[X_TAIL + half // 2, :, (half % 2) * 128 : (half % 2) * 128 + 128]
        rows.append(jnp.concatenate([ref[g], pltpu.roll(tile, (120 - 16 * j) % 128, 1)], axis=1) if (120 - 16 * j) % 128 else jnp.concatenate([ref[g], tile], axis=1))
    return jnp.concatenate(rows, axis=0)


def block_kernel(
    u_ref, k_ref, f_ref, up_ref, down_ref, z_ref,
    uo_ref, ko_ref, k_in_ref, r_in_ref, rc_ref, kc_ref, chip_ref, link_ref,
    ue_ref, ke_ref, fe_ref, tmp_ref,
):
    gz, cy, core = lax.axis_index("gz"), lax.axis_index("coarse"), lax.rem(lax.axis_index("pencil"), 2)
    lane = lanes((RE, 128))
    sides = []
    for from_z, inside in ((3, gz > 0), (1, gz < 3)):
        z = lax.rem(gz + from_z, 4) * 4
        rows = [
            z_ref[z + cy],
            jnp.where(cy < 3, z_ref[z + lax.rem(cy + 1, 4), :H], 0.0),
            jnp.where(cy > 0, z_ref[z + lax.rem(cy + 3, 4), :H], 0.0),
        ]
        sides.append(jnp.where(inside, jnp.concatenate(rows, axis=0), 0.0))
    for i, (own, ext) in enumerate(((u_ref, ue_ref), (k_ref, ke_ref), (f_ref, fe_ref))):
        scale = (lambda v: 0.5 * v) if i == 1 else (lambda v: v)
        for p in range(NX):
            g = i * NX + p
            t, q = divmod(g, 16)
            before, after = (side[:, t * 128 : t * 128 + 128] for side in sides)
            if (120 - H * q) % 128:
                before = pltpu.roll(before, (120 - H * q) % 128, 1)
            if q:
                after = pltpu.roll(after, 128 - H * q, 1)
            ext[p, :NY, :NZ] = scale(own[p])
            ext[p, NY : NY + H, :NZ] = scale(down_ref[g])
            ext[p, NY + H :, :NZ] = scale(up_ref[g])
            ext[p, :, NZ:] = scale(jnp.where(lane < H, after, jnp.where(lane >= 120, before, 0.0)))
    even = lanes((RE, ZE)) % 2 == 0
    flux_x = None
    r_pair = k_pair = None
    for p in range(NX):
        k, u = ke_ref[p], ue_ref[p]
        flux = (k + up(k, 1)) * (u - up(u, 1))
        out = flux - down(flux, 1)
        flux = (k + up(k, 0)) * (u - up(u, 0))
        out = out + (flux - down(flux, 0))
        if flux_x is not None:
            out = out - flux_x
        if p < NX - 1:
            flux_x = (k + ke_ref[p + 1]) * (u - ue_ref[p + 1])
            out = out + flux_x
        r = fe_ref[p] - out
        q = place(core, p, NX)
        r_in_ref[q] = inner_rows(r)
        k_in_ref[q] = inner_rows(k)
        if p % 2 == 0:
            r_pair, k_pair = r, k
        else:
            c = place(core, p // 2, CX)
            rc_ref[c] = restrict_plane(r_pair + r, tmp_ref.at[p - 1], even, 0.125)
            kc_ref[c] = restrict_plane(k_pair + k, tmp_ref.at[p], even, 0.03125)
    for i in range(2):
        end = place(core, i * (NX - 1), NX)
        uo_ref[i], ko_ref[i] = ue_ref[end], ke_ref[end]
    even_c = lanes((CE, ZE)) % 2 == 0
    for i, ref in enumerate((link_ref, chip_ref)):
        at, step, c = i * (NX - 1), 1 - 2 * i, i * (CX - 1)
        tails = {}
        send_rows(ref, tails, X_U, uo_ref[i])
        send_rows(ref, tails, X_K, ko_ref[i])
        send_rows(ref, tails, X_K2, k_in_ref[at + step])
        send_rows(ref, tails, X_K3, k_in_ref[at + 2 * step, :NY])
        send_rows(ref, tails, X_R1, r_in_ref[at])
        send_rows(ref, tails, X_R2, r_in_ref[at + step, :NY])
        for d in range(CX):
            both = jnp.where(even_c, rc_ref[c + d * step], kc_ref[c + d * step])
            send_rows(ref, tails, X_C + 2 * d, both if d < 3 else both[:CY])
        send_tails(ref, tails)


def faces_yz(k, by=1):
    ky, kz = k + up(k, 0), k + up(k, 1, by)
    return ky, kz, (ky + down(ky, 0)) + (kz + down(kz, 1, by))


def flux_yz(v, ky, kz, by=1):
    flux = kz * (v - up(v, 1, by))
    out = flux - down(flux, 1, by)
    flux = ky * (v - up(v, 0))
    return out + (flux - down(flux, 0))


def inverse(k, diag, scale=1.0):
    return jnp.where(k > 0.0, scale / diag, 0.0)


def step_d1(r1, d0, inv):
    return (RHO1 * RHO0) * d0 + (2.0 * RHO1 / DELTA) * (r1 * inv)


def main(v):
    return v[:NY, :NZ]


def open_message(msg, u_end, k_end, r_end, rc_end, tmp_ref):
    even, even_c = lanes((RE, ZE)) % 2 == 0, lanes((CE, ZE)) % 2 == 0
    none = jnp.zeros((RF - NY, ZE), f32)
    un, kn = received_rows(msg, X_U, 4), received_rows(msg, X_K, 4)
    flux = (k_end + kn) * (u_end - un)
    inner = inner_rows(flux)
    coarse = restrict_plane(flux, tmp_ref, even, 0.125)
    ks = [inner_rows(kn), received_rows(msg, X_K2, 3)]
    ks.append(jnp.concatenate([received_rows(msg, X_K3, 2), none], axis=0))
    rs = [received_rows(msg, X_R1, 3) + inner]
    rs.append(jnp.concatenate([received_rows(msg, X_R2, 2), none], axis=0))
    kcs, rcs = [], []
    for d in range(CX):
        if d < 3:
            both = received_rows(msg, X_C + 2 * d, 2)
            rc = jnp.where(even_c, both, down(both, 1))
            rcs.append(rc + coarse if d == 0 else rc)
        else:
            both = jnp.concatenate([received_rows(msg, X_C + 2 * d, 1), none], axis=0)
        kcs.append(jnp.where(even_c, up(both, 1), both))
    return r_end - inner, ks, rs, rc_end - coarse, kcs, rcs


OFF, COFF = 3, 4


def at(near, own, s, first, inward, off=OFF):
    return own[inward(s)] if s >= first else near[off + s]


def fine_side(opened, inward, own, near, emit):
    r_end, ks, rs = opened[:3]
    k, r, ky, kz, inv, d0, r1, d1 = own
    k_x, r_x, ky_x, kz_x, inv_x, d0_x, d1_x = near
    for d, plane in enumerate(ks):
        k_x[OFF - 1 - d] = plane
    for d, plane in enumerate([r_end] + rs):
        r_x[OFF - d] = plane

    def k_at(s):
        return at(k_x, k, s, 0, inward)

    def d0_at(s):
        return at(d0_x, d0, s, 1, inward)

    def d1_at(s):
        return at(d1_x, d1, s, 2, inward)

    def faces_at(s):
        return at(ky_x, ky, s, 0, inward), at(kz_x, kz, s, 0, inward)

    kx = k_at(-3) + k_at(-2)
    for s in range(-2, 1):
        kv = k_at(s)
        before, kx = kx, kv + k_at(s + 1)
        if s < 0:
            ky_x[OFF + s], kz_x[OFF + s], diag = faces_yz(kv)
            diag = diag + before + kx
        else:
            diag = inv[inward(0)] + before
        scale = inverse(kv, diag)
        inv_x[OFF + s] = scale
        d0_x[OFF + s] = r_x[OFF + s] * scale * (1.0 / THETA)
    flux_x = (k_at(-2) + k_at(-1)) * (d0_at(-2) - d0_at(-1))
    for s in range(-1, 2):
        v = d0_at(s)
        out = flux_yz(v, *faces_at(s)) - flux_x
        flux_x = (k_at(s) + k_at(s + 1)) * (v - d0_at(s + 1))
        rv = at(r_x, r, s, 1, inward) - (out + flux_x)
        r_x[OFF + s] = rv
        d1_x[OFF + s] = step_d1(rv, v, at(inv_x, inv, s, 1, inward))
    flux_x = main((k_at(-1) + k_at(0)) * (d1_at(-1) - d1_at(0)))
    for s in range(3):
        v = d1_at(s)
        out = main(flux_yz(v, *faces_at(s))) - flux_x
        flux_x = main((k_at(s) + k_at(s + 1)) * (v - d1_at(s + 1)))
        rest = main(at(r_x, r1, s, 2, inward)) - (out + flux_x)
        emit(s, rest, main(d0_at(s)) + main(v) if s < 2 else None)


def coarse_side(opened, inward, kc, cinv, near):
    rc_end, kcs, rcs = opened[3:]
    q_x, s_x, cy_x, cz_x, cinv_x, e0_x = near
    for d, plane in enumerate(kcs):
        q_x[COFF - 1 - d] = plane
    for d, plane in enumerate([rc_end] + rcs):
        s_x[COFF - d] = plane
    kx = q_x[COFF - 4] + q_x[COFF - 3]
    for s in range(-3, 1):
        k = at(q_x, kc, s, 0, inward, COFF)
        before, kx = kx, k + at(q_x, kc, s + 1, 0, inward, COFF)
        if s < 0:
            cy_x[COFF + s], cz_x[COFF + s], diag = faces_yz(k, 2)
            diag = diag + before + kx
        else:
            diag = cinv[inward(0)] + before
        scale = inverse(k, diag, 0.8)
        cinv_x[COFF + s] = scale
        e0_x[COFF + s] = s_x[COFF + s] * scale


def sweep(first, last, e_at, q_at, rc_at, cy_at, cz_at, cinv_at, emit):
    flux_x = (q_at(first - 1) + q_at(first)) * (e_at(first - 1) - e_at(first))
    for c in range(first, last + 1):
        e = e_at(c)
        out = flux_yz(e, cy_at(c), cz_at(c), 2) - flux_x
        flux_x = (q_at(c) + q_at(c + 1)) * (e - e_at(c + 1))
        emit(c, e + cinv_at(c) * (rc_at(c) - (out + flux_x)))


def mid_kernel(
    u_ref, k_ref, r_ref, rc_ref, kc_ref,
    ky_ref, kz_ref, inv_ref, d0_ref, r1_ref, d1_ref, sum_ref, smooth_ref,
    cy_ref, cz_ref, cinv_ref, e0_ref,
):
    core = lax.rem(lax.axis_index("pencil"), 2)
    kx = None
    for p in range(NX):
        k = k_ref[p]
        ky_ref[p], kz_ref[p], diag = faces_yz(k)
        if kx is not None:
            diag = diag + kx
        if p < NX - 1:
            kx = k + k_ref[p + 1]
            diag = diag + kx
        if 0 < p < NX - 1:
            inv = inverse(k, diag)
            inv_ref[p] = inv
            d0_ref[p] = r_ref[p] * inv * (1.0 / THETA)
        else:
            inv_ref[p] = diag
    flux_x = (k_ref[1] + k_ref[2]) * (d0_ref[1] - d0_ref[2])
    for p in range(2, NX - 2):
        d0 = d0_ref[p]
        out = flux_yz(d0, ky_ref[p], kz_ref[p]) - flux_x
        flux_x = (k_ref[p] + k_ref[p + 1]) * (d0 - d0_ref[p + 1])
        r1 = r_ref[p] - (out + flux_x)
        d1 = step_d1(r1, d0, inv_ref[p])
        r1_ref[p], d1_ref[p] = r1, d1
        sum_ref[p] = u_ref[place(core, p, NX)] + main(d0) + main(d1)
    flux_x = main((k_ref[2] + k_ref[3]) * (d1_ref[2] - d1_ref[3]))
    for p in range(3, NX - 3):
        d1 = d1_ref[p]
        out = main(flux_yz(d1, ky_ref[p], kz_ref[p])) - flux_x
        flux_x = main((k_ref[p] + k_ref[p + 1]) * (d1 - d1_ref[p + 1]))
        smooth_ref[p] = main(r1_ref[p]) - (out + flux_x)
    kx = None
    for c in range(CX):
        k = kc_ref[c]
        cy_ref[c], cz_ref[c], diag = faces_yz(k, 2)
        if kx is not None:
            diag = diag + kx
        if c < CX - 1:
            kx = k + kc_ref[c + 1]
            diag = diag + kx
        if 0 < c < CX - 1:
            inv = inverse(k, diag, 0.8)
            cinv_ref[c] = inv
            e0_ref[c] = rc_ref[c] * inv
        else:
            cinv_ref[c] = diag


def chip_kernel(
    u_ref, uo_ref, ko_ref, k_ref, r_ref, rc_ref, kc_ref,
    ky_ref, kz_ref, inv_ref, d0_ref, r1_ref, d1_ref,
    cy_ref, cz_ref, cinv_ref, e0_ref, msg_ref,
    sum_ref, smooth_ref, q_x, s_x, cinv_x, e1_x, e2_x,
    k_x, r_x, ky_x, kz_x, inv_x, d0_x, d1_x, cy_x, cz_x, e0_x, tmp_ref,
):
    core = lax.rem(lax.axis_index("pencil"), 2)
    opened = open_message(msg_ref, uo_ref[1], ko_ref[1], r_ref[NX - 1], rc_ref[CX - 1], tmp_ref)

    def emit(s, rest, step):
        smooth_ref[s] = rest
        if s < 2:
            sum_ref[s] = u_ref[place(core, NX - 1 - s, NX)] + step

    fine_side(
        opened, lambda s: NX - 1 - s,
        (k_ref, r_ref, ky_ref, kz_ref, inv_ref, d0_ref, r1_ref, d1_ref),
        (k_x, r_x, ky_x, kz_x, inv_x, d0_x, d1_x), emit,
    )

    def inward(s):
        return CX - 1 - s

    coarse_side(opened, inward, kc_ref, cinv_ref, (q_x, s_x, cy_x, cz_x, cinv_x, e0_x))

    def pick(near, own, first):
        return lambda s: at(near, own, s, first, inward, COFF)

    rest = (
        pick(q_x, kc_ref, 0), pick(s_x, rc_ref, 1), pick(cy_x, cy_ref, 0), pick(cz_x, cz_ref, 0),
        pick(cinv_x, cinv_ref, 1),
    )

    def keep(ref):
        def store(s, e):
            ref[COFF + s] = e

        return store

    sweep(-2, 1, pick(e0_x, e0_ref, 1), *rest, keep(e1_x))
    sweep(-1, 0, lambda s: e1_x[COFF + s], *rest, keep(e2_x))


def final_kernel(
    u_ref, uo_ref, ko_ref, k_ref, r_ref, rc_ref, kc_ref,
    ky_ref, kz_ref, inv_ref, d0_ref, r1_ref, d1_ref, sum_ref, smooth_ref,
    cy_ref, cz_ref, cinv_ref, e0_ref,
    sum_c, smooth_c, q_c, s_c, cinv_c, e1_c, e2_c, msg_ref,
    new_hbm, smooth_hbm,
    k_x, r_x, ky_x, kz_x, inv_x, d0_x, d1_x, q_x, s_x, cy_x, cz_x, cinv_x, e0_x, e1_x, e2_x,
    tmp_ref, lift_ref, new_ref, out_ref, new_sem, smooth_sem,
):
    core = lax.rem(lax.axis_index("pencil"), 2)
    copies = []

    def put(src, dst, sem, p):
        copies.append(pltpu.make_async_copy(src, dst.at[place(core, p, NX)], sem.at[p]))
        copies[-1].start()

    for p in range(3, NX):
        put(smooth_ref.at[p] if p < NX - 3 else smooth_c.at[NX - 1 - p], smooth_hbm, smooth_sem, p)
    opened = open_message(msg_ref, uo_ref[0], ko_ref[0], r_ref[0], rc_ref[0], tmp_ref)

    def emit(p, rest, step):
        out_ref[p] = rest
        put(out_ref.at[p], smooth_hbm, smooth_sem, p)
        if p < 2:
            new_ref[p] = u_ref[place(core, p, NX)] + step

    fine_side(
        opened, lambda s: s,
        (k_ref, r_ref, ky_ref, kz_ref, inv_ref, d0_ref, r1_ref, d1_ref),
        (k_x, r_x, ky_x, kz_x, inv_x, d0_x, d1_x), emit,
    )
    coarse_side(opened, lambda s: s, kc_ref, cinv_ref, (q_x, s_x, cy_x, cz_x, cinv_x, e0_x))

    def pick(near, own, first, far=None, beyond=CX):
        def read(c):
            if c < first:
                return near[COFF + c]
            return own[c] if c < beyond else far[COFF + CX - 1 - c]

        return read

    rest = (
        pick(q_x, kc_ref, 0, q_c), pick(s_x, rc_ref, 1, s_c, 3), pick(cy_x, cy_ref, 0),
        pick(cz_x, cz_ref, 0), pick(cinv_x, cinv_ref, 1, cinv_c, 3),
    )

    def keep(ref):
        def store(c, e):
            ref[COFF + c] = e

        return store

    def lift(c, e):
        cols = []
        for t in range(NZ // 128):
            part = e[:CY, t * 128 : (t + 1) * 128]
            tile = lift_ref.at[2 * c + t]
            tile[pl.ds(0, CY, stride=2), :] = part
            tile[pl.ds(1, CY, stride=2), :] = part
            cols.append(tile[...])
        lifted = jnp.concatenate(cols, axis=1)
        for p in (2 * c, 2 * c + 1):
            if p < 2:
                done = new_ref[p]
            else:
                done = sum_ref[p] if p < NX - 2 else sum_c[NX - 1 - p]
            new_ref[p] = done + lifted
            put(new_ref.at[p], new_hbm, new_sem, p)

    sweep(-2, 1, pick(e0_x, e0_ref, 1), *rest, keep(e1_x))
    sweep(-1, 2, pick(e1_x, None, 2, e1_c, 2), *rest, keep(e2_x))
    sweep(0, 3, pick(e2_x, None, 3, e2_c, 3), *rest, lift)
    for copy in copies:
        copy.wait()


def call(kernel, outs, specs, scratch, bytes_accessed, flops):
    spaces = {"s": pltpu.SMEM, "v": pltpu.VMEM, "h": pltpu.HBM}
    return pl.pallas_call(
        kernel,
        out_shape=[jax.ShapeDtypeStruct(tuple(s), f32) for s in outs],
        in_specs=[pl.BlockSpec(memory_space=spaces[s]) for s in specs],
        out_specs=[
            pl.BlockSpec(memory_space=pl.ANY if isinstance(s, list) else pltpu.VMEM) for s in outs
        ],
        scratch_shapes=[pltpu.VMEM(s, f32) if isinstance(s, tuple) else s for s in scratch],
        compiler_params=pltpu.CompilerParams(vmem_limit_bytes=16 << 20),
        cost_estimate=pl.CostEstimate(flops=flops, bytes_accessed=bytes_accessed, transcendentals=0),
    )


def shifted(cells, axis, by):
    count = lax.axis_size(axis)
    return lax.ppermute(cells, axis, [(i, i + by) for i in range(count) if 0 <= i + by < count])


def swapped(cells, axis, first):
    count = lax.axis_size(axis)
    pairs = []
    for i in range(first, count - 1, 2):
        pairs += [(i, i + 1), (i + 1, i)]
    return lax.ppermute(cells, axis, pairs)


def on_device(right_side, conductivity, guess):
    own = (NX, NY, NZ)
    dma = pltpu.SemaphoreType.DMA
    u, k, f, upward, downward, ends = call(
        pack_kernel,
        [own, own, own, (GROUPS, H, NZ), (GROUPS, H, NZ), [16, NY, 256]],
        "hhh", [(2, NY, 256), dma((6,)), dma((6,))], 1 << 20, 1 << 18,
    )(*(pltpu.with_memory_space_constraint(a, pltpu.HBM) for a in (guess, conductivity, right_side)))
    upward = shifted(upward, "coarse", 1)
    downward = shifted(downward, "coarse", -1)
    ends = lax.all_to_all(ends, ("gz", "coarse"), 0, 0)

    def fine(n):
        return (n, RF, ZE)

    def coarse(n):
        return (n, CE, ZE)

    message = (X_GROUPS + 2, 8, NZ)
    uo, ko, k_in, r_in, rc, kc, chip, link = call(
        block_kernel,
        [(2, RE, ZE), (2, RE, ZE), fine(NX), fine(NX), coarse(CX), coarse(CX), message, message],
        "vvvvvv", [(NX, RE, ZE)] * 3 + [(NX, ZE // 128, RE, 128)], 3 << 20, 1 << 22,
    )(u, k, f, upward, downward, ends)
    chip = swapped(chip, "pencil", 0)
    link = swapped(link, "pencil", 1)
    edges = (ZE // 128, RE, 128)
    *fine_own, sums, smooth, cy, cz, cinv, e0 = call(
        mid_kernel, [fine(NX)] * 6 + [own, own] + [coarse(CX)] * 4, "v" * 5, [],
        4 << 20, 1 << 22,
    )(u, k_in, r_in, rc, kc)
    half = call(
        chip_kernel,
        [(2, NY, NZ), (3, NY, NZ)] + [coarse(5)] * 3 + [coarse(6)] * 2, "v" * 18,
        [fine(3), fine(5)] + [fine(5)] * 5 + [coarse(5)] * 3 + [edges], 4 << 20, 1 << 22,
    )(u, uo, ko, k_in, r_in, rc, kc, *fine_own, cy, cz, cinv, e0, chip)
    return tuple(
        call(
            final_kernel, [list(own), list(own)], "v" * 27,
            [fine(3), fine(5)] + [fine(5)] * 5 + [coarse(5)] * 6 + [coarse(6), coarse(7)]
            + [edges, (NX, NY, 128), own, (3, NY, NZ), dma((NX,)), dma((NX,))],
            4 << 20, 1 << 22,
        )(u, uo, ko, k_in, r_in, rc, kc, *fine_own, sums, smooth, cy, cz, cinv, e0, *half, link)
    )


def solution(mesh):
    spec = P("pencil", "coarse", "gz")
    return jax.shard_map(
        on_device,
        mesh=mesh,
        in_specs=(spec, spec, spec),
        out_specs=(spec, spec),
        check_vma=False,
    )
```

```python
import jax
import jax.numpy as jnp
from jax import lax
from jax.experimental import pallas as pl
from jax.experimental.pallas import tpu as pltpu
from jax.sharding import PartitionSpec as P


THETA = 1.1
DELTA = 0.8
SIGMA = THETA / DELTA
RHO0 = 1.0 / SIGMA
RHO1 = 1.0 / (2.0 * SIGMA - RHO0)

NX, NY, NZ = 8, 16, 256
H = 8
RE = NY + 2 * H
RF = NY + H
ZE = NZ + 128
CX, CY = NX // 2, NY // 2
CE = RE // 2
GROUPS = 3 * NX
f32 = jnp.float32


def up(v, axis, by=1):
    return pltpu.roll(v, v.shape[axis] - by, axis)


def down(v, axis, by=1):
    return pltpu.roll(v, by, axis)


def lanes(shape):
    return lax.broadcasted_iota(jnp.int32, shape, len(shape) - 1)


def pack_kernel(
    u_hbm, k_hbm, f_hbm,
    u_ref, k_ref, f_ref, up_ref, down_ref, z_hbm,
    end_ref, own_sem, end_sem,
):
    gz, cy = lax.axis_index("gz"), lax.axis_index("coarse")
    fields = (u_ref, k_ref, f_ref)
    copies = []
    for i, (far, near) in enumerate(zip((u_hbm, k_hbm, f_hbm), fields)):
        for half in range(2):
            at = pl.ds(half * NX // 2, NX // 2)
            copies.append(pltpu.make_async_copy(far.at[at], near.at[at], own_sem.at[2 * i + half]))
            copies[-1].start()
    for copy in copies:
        copy.wait()
    group = lanes((NY, 128)) // H
    sends = []
    for side, (first, start, to_z) in enumerate(((NZ - 128, H, 1), (0, 0, 3))):
        for t in range(2):
            tile = jnp.zeros((NY, 128), f32)
            for q in range(16):
                g = t * 16 + q
                if g < GROUPS:
                    cells = fields[g // NX][g % NX, :, first : first + 128]
                    shift = (H * q + start) % 128
                    moved = pltpu.roll(cells, shift, 1) if shift else cells
                    tile = jnp.where(group == q, moved, tile)
            end_ref[side, :, t * 128 : (t + 1) * 128] = tile
        z = lax.rem(gz + to_z, 4) * 4
        end = end_ref.at[side]
        for j, (src, dst) in enumerate((
            (end, z_hbm.at[z + cy]),
            (end.at[pl.ds(NY - H, H)], z_hbm.at[z + lax.rem(cy + 1, 4), pl.ds(0, H)]),
            (end.at[pl.ds(0, H)], z_hbm.at[z + lax.rem(cy + 3, 4), pl.ds(0, H)]),
        )):
            sends.append(pltpu.make_async_copy(src, dst, end_sem.at[3 * side + j]))
            sends[-1].start()
    for i, field in enumerate(fields):
        for p in range(NX):
            up_ref[i * NX + p] = field[p, NY - H :, :]
            down_ref[i * NX + p] = field[p, :H, :]
    for copy in sends:
        copy.wait()


def lane_pairs(plane, even):
    return plane + jnp.where(even, up(plane, 1), down(plane, 1))


def restrict_plane(plane, scratch_ref, even, scale):
    rows, cols = plane.shape[0], []
    for t in range(ZE // 128):
        tile = scratch_ref.at[t]
        tile[:rows] = plane[:, t * 128 : (t + 1) * 128]
        cols.append(tile[pl.ds(0, rows // 2, stride=2), :] + tile[pl.ds(1, rows // 2, stride=2), :])
    return scale * lane_pairs(jnp.concatenate(cols, axis=1), even)


def place(core, p, count):
    return core * (count - 1) + (1 - 2 * core) * p


def inner_rows(plane):
    row = lax.broadcasted_iota(jnp.int32, (H, ZE), 0)
    return jnp.concatenate(
        [plane[:NY], jnp.where(row < H // 2, plane[NY : NY + H], plane[NY + H :])], axis=0
    )


X_U, X_K, X_K2, X_K3, X_R1, X_R2, X_C = 0, 4, 8, 11, 13, 16, 18
X_GROUPS = X_C + 3 * 2 + 1
X_TAIL = X_GROUPS


def send_rows(ref, tails, first, plane):
    for j in range(plane.shape[0] // 8):
        rows = plane[j * 8 : (j + 1) * 8]
        ref[first + j] = rows[:, :NZ]
        tails[first + j] = rows[:, NZ:]


def send_tails(ref, tails):
    lane = lanes((8, 128)) // 16
    for half in range(4):
        tile = jnp.zeros((8, 128), f32)
        for j in range(8):
            g = half * 8 + j
            if g < X_GROUPS:
                shift = (16 * j + 8) % 128
                tile = jnp.where(lane == j, pltpu.roll(tails[g], shift, 1), tile)
        ref[X_TAIL + half // 2, :, (half % 2) * 128 : (half % 2) * 128 + 128] = tile


def received_rows(ref, first, groups):
    rows = []
    for g in range(first, first + groups):
        half, j = divmod(g, 8)
        tile = ref[X_TAIL + half // 2, :, (half % 2) * 128 : (half % 2) * 128 + 128]
        rows.append(jnp.concatenate([ref[g], pltpu.roll(tile, (120 - 16 * j) % 128, 1)], axis=1) if (120 - 16 * j) % 128 else jnp.concatenate([ref[g], tile], axis=1))
    return jnp.concatenate(rows, axis=0)


def own_kernel(
    u_ref, k_ref, f_ref, z_ref,
    uo_ref, ko_ref, ro_ref, rc_ref, kc_ref, zu_ref, zk_ref, zf_ref,
    tmp_ref,
):
    gz, cy = lax.axis_index("gz"), lax.axis_index("coarse")
    lane = lanes((RE, 128))
    sides = []
    for from_z, inside in ((3, gz > 0), (1, gz < 3)):
        z = lax.rem(gz + from_z, 4) * 4
        rows = [
            z_ref[z + cy],
            jnp.where(cy < 3, z_ref[z + lax.rem(cy + 1, 4), :H], 0.0),
            jnp.where(cy > 0, z_ref[z + lax.rem(cy + 3, 4), :H], 0.0),
        ]
        sides.append(jnp.where(inside, jnp.concatenate(rows, axis=0), 0.0))

    def extended(i, p, own, halo):
        t, q = divmod(i * NX + p, 16)
        before, after = (side[:, t * 128 : t * 128 + 128] for side in sides)
        if (120 - H * q) % 128:
            before = pltpu.roll(before, (120 - H * q) % 128, 1)
        if q:
            after = pltpu.roll(after, 128 - H * q, 1)
        beyond = jnp.where(lane < H, after, jnp.where(lane >= 120, before, 0.0))
        cells = own[p]
        if i == 1:
            beyond, cells = 0.5 * beyond, 0.5 * cells
        halo[p] = beyond[NY:]
        return jnp.concatenate([cells, beyond[:NY]], axis=1)

    even = lanes((CY, ZE)) % 2 == 0
    inner = lax.broadcasted_iota(jnp.int32, (NY, ZE), 0) < NY - 1
    flux_x = r_pair = k_pair = None
    u, k = extended(0, 0, u_ref, zu_ref), extended(1, 0, k_ref, zk_ref)
    for p in range(NX):
        uo_ref[p], ko_ref[p] = u, k
        flux = (k + up(k, 1)) * (u - up(u, 1))
        out = flux - down(flux, 1)
        flux = jnp.where(inner, (k + up(k, 0)) * (u - up(u, 0)), 0.0)
        out = out + (flux - down(flux, 0))
        if flux_x is not None:
            out = out - flux_x
        r, k_now = extended(2, p, f_ref, zf_ref), k
        if p < NX - 1:
            un, kn = extended(0, p + 1, u_ref, zu_ref), extended(1, p + 1, k_ref, zk_ref)
            flux_x = (k + kn) * (u - un)
            out = out + flux_x
            u, k = un, kn
        r = r - out
        ro_ref[p] = r
        if p % 2 == 0:
            r_pair, k_pair = r, k_now
        else:
            rc_ref[p // 2] = restrict_plane(r_pair + r, tmp_ref.at[p - 1], even, 0.125)
            kc_ref[p // 2] = restrict_plane(k_pair + k_now, tmp_ref.at[p], even, 0.03125)


def edge_kernel(
    u_ref, k_ref, r_ref, rcl_ref, kcl_ref, zu_ref, zk_ref, zf_ref, up_ref, down_ref,
    uo_ref, ko_ref, k_in_ref, r_in_ref, rc_ref, kc_ref, chip_ref, link_ref,
    tmp_ref,
):
    core = lax.rem(lax.axis_index("pencil"), 2)
    row = lax.broadcasted_iota(jnp.int32, (H, ZE), 0)
    even = lanes((CY, ZE)) % 2 == 0

    def halo(i, p, beyond):
        g = i * NX + p
        scale = (lambda v: 0.5 * v) if i == 1 else (lambda v: v)
        cells = jnp.concatenate([scale(down_ref[g]), scale(up_ref[g])], axis=0)
        return jnp.concatenate([cells, beyond[p]], axis=1)

    flux_x = r_pair = k_pair = d_pair = None
    u, k = halo(0, 0, zu_ref), halo(1, 0, zk_ref)
    for p in range(NX):
        own_u, own_k, own_r = u_ref[p], k_ref[p], r_ref[p]
        flux = (k + up(k, 1)) * (u - up(u, 1))
        out = flux - down(flux, 1)
        kl, ul, kv, uv = k[:H], u[:H], k[H:], u[H:]
        low = (down(own_k[H:], 0) + kl) * (down(own_u[H:], 0) - ul)
        high = (kv + up(own_k[:H], 0)) * (uv - up(own_u[:H], 0))
        flux = (kl + up(kl, 0)) * (ul - up(ul, 0))
        below = flux - jnp.where(row == 0, low, down(flux, 0))
        flux = jnp.where(row == H - 1, high, (kv + up(kv, 0)) * (uv - up(uv, 0)))
        out = out + jnp.concatenate([below, flux - down(flux, 0)], axis=0)
        first = jnp.where(row == 0, down(high, 0), 0.0)
        last = jnp.where(row == H - 1, up(low, 0), 0.0)
        if flux_x is not None:
            out = out - flux_x
        r, k_now, u_now = halo(2, p, zf_ref), k, u
        if p < NX - 1:
            un, kn = halo(0, p + 1, zu_ref), halo(1, p + 1, zk_ref)
            flux_x = (k + kn) * (u - un)
            out = out + flux_x
            u, k = un, kn
        r = r - out
        q = place(core, p, NX)
        near = row < H // 2
        r_in_ref[q] = jnp.concatenate(
            [own_r[:H] + first, own_r[H:] - last, jnp.where(near, r[:H], r[H:])], axis=0
        )
        k_in_ref[q] = jnp.concatenate([own_k, jnp.where(near, k_now[:H], k_now[H:])], axis=0)
        if p in (0, NX - 1):
            end = place(core, p // (NX - 1), 2)
            uo_ref[end] = jnp.concatenate([own_u, u_now], axis=0)
            ko_ref[end] = jnp.concatenate([own_k, k_now], axis=0)
        if p % 2 == 0:
            r_pair, k_pair, d_pair = r, k_now, first - last
        else:
            c = place(core, p // 2, CX)
            rc_ref[c] = jnp.concatenate([
                rcl_ref[p // 2] + 0.125 * lane_pairs(d_pair + (first - last), even),
                restrict_plane(r_pair + r, tmp_ref.at[p - 1], even, 0.125),
            ], axis=0)
            kc_ref[c] = jnp.concatenate(
                [kcl_ref[p // 2], restrict_plane(k_pair + k_now, tmp_ref.at[p], even, 0.03125)], axis=0
            )
    even_c = lanes((CE, ZE)) % 2 == 0
    for i, ref in enumerate((link_ref, chip_ref)):
        at, step, c = i * (NX - 1), 1 - 2 * i, i * (CX - 1)
        tails = {}
        send_rows(ref, tails, X_U, uo_ref[i])
        send_rows(ref, tails, X_K, ko_ref[i])
        send_rows(ref, tails, X_K2, k_in_ref[at + step])
        send_rows(ref, tails, X_K3, k_in_ref[at + 2 * step, :NY])
        send_rows(ref, tails, X_R1, r_in_ref[at])
        send_rows(ref, tails, X_R2, r_in_ref[at + step, :NY])
        for d in range(CX):
            both = jnp.where(even_c, rc_ref[c + d * step], kc_ref[c + d * step])
            send_rows(ref, tails, X_C + 2 * d, both if d < 3 else both[:CY])
        send_tails(ref, tails)


def faces_yz(k, by=1):
    ky, kz = k + up(k, 0), k + up(k, 1, by)
    return ky, kz, (ky + down(ky, 0)) + (kz + down(kz, 1, by))


def flux_yz(v, ky, kz, by=1):
    flux = kz * (v - up(v, 1, by))
    out = flux - down(flux, 1, by)
    flux = ky * (v - up(v, 0))
    return out + (flux - down(flux, 0))


def inverse(k, diag, scale=1.0):
    return jnp.where(k > 0.0, scale / diag, 0.0)


def step_d1(r1, d0, inv):
    return (RHO1 * RHO0) * d0 + (2.0 * RHO1 / DELTA) * (r1 * inv)


def main(v):
    return v[:NY, :NZ]


def open_message(msg, u_end, k_end, r_end, rc_end, tmp_ref):
    even_c = lanes((CE, ZE)) % 2 == 0
    none = jnp.zeros((RF - NY, ZE), f32)
    un, kn = received_rows(msg, X_U, 4), received_rows(msg, X_K, 4)
    flux = (k_end + kn) * (u_end - un)
    inner = inner_rows(flux)
    coarse = restrict_plane(flux, tmp_ref, even_c, 0.125)
    ks = [inner_rows(kn), received_rows(msg, X_K2, 3)]
    ks.append(jnp.concatenate([received_rows(msg, X_K3, 2), none], axis=0))
    rs = [received_rows(msg, X_R1, 3) + inner]
    rs.append(jnp.concatenate([received_rows(msg, X_R2, 2), none], axis=0))
    kcs, rcs = [], []
    for d in range(CX):
        if d < 3:
            both = received_rows(msg, X_C + 2 * d, 2)
            rc = jnp.where(even_c, both, down(both, 1))
            rcs.append(rc + coarse if d == 0 else rc)
        else:
            both = jnp.concatenate([received_rows(msg, X_C + 2 * d, 1), none], axis=0)
        kcs.append(jnp.where(even_c, up(both, 1), both))
    return r_end - inner, ks, rs, rc_end - coarse, kcs, rcs


OFF, COFF = 3, 4


def at(near, own, s, first, inward, off=OFF):
    return own[inward(s)] if s >= first else near[off + s]


def fine_side(opened, inward, own, near, emit):
    r_end, ks, rs = opened[:3]
    k, r, ky, kz, inv, d0, r1, d1 = own
    k_x, r_x, ky_x, kz_x, inv_x, d0_x, d1_x = near
    for d, plane in enumerate(ks):
        k_x[OFF - 1 - d] = plane
    for d, plane in enumerate([r_end] + rs):
        r_x[OFF - d] = plane

    def k_at(s):
        return at(k_x, k, s, 0, inward)

    def d0_at(s):
        return at(d0_x, d0, s, 1, inward)

    def d1_at(s):
        return at(d1_x, d1, s, 2, inward)

    def faces_at(s):
        return at(ky_x, ky, s, 0, inward), at(kz_x, kz, s, 0, inward)

    kx = k_at(-3) + k_at(-2)
    for s in range(-2, 1):
        kv = k_at(s)
        before, kx = kx, kv + k_at(s + 1)
        if s < 0:
            ky_x[OFF + s], kz_x[OFF + s], diag = faces_yz(kv)
            diag = diag + before + kx
        else:
            diag = inv[inward(0)] + before
        scale = inverse(kv, diag)
        inv_x[OFF + s] = scale
        d0_x[OFF + s] = r_x[OFF + s] * scale * (1.0 / THETA)
    flux_x = (k_at(-2) + k_at(-1)) * (d0_at(-2) - d0_at(-1))
    for s in range(-1, 2):
        v = d0_at(s)
        out = flux_yz(v, *faces_at(s)) - flux_x
        flux_x = (k_at(s) + k_at(s + 1)) * (v - d0_at(s + 1))
        rv = at(r_x, r, s, 1, inward) - (out + flux_x)
        r_x[OFF + s] = rv
        d1_x[OFF + s] = step_d1(rv, v, at(inv_x, inv, s, 1, inward))
    flux_x = main((k_at(-1) + k_at(0)) * (d1_at(-1) - d1_at(0)))
    for s in range(3):
        v = d1_at(s)
        out = main(flux_yz(v, *faces_at(s))) - flux_x
        flux_x = main((k_at(s) + k_at(s + 1)) * (v - d1_at(s + 1)))
        rest = main(at(r_x, r1, s, 2, inward)) - (out + flux_x)
        emit(s, rest, main(d0_at(s)) + main(v) if s < 2 else None)


def coarse_side(opened, inward, kc, cinv, near):
    rc_end, kcs, rcs = opened[3:]
    q_x, s_x, cy_x, cz_x, cinv_x, e0_x = near
    for d, plane in enumerate(kcs):
        q_x[COFF - 1 - d] = plane
    for d, plane in enumerate([rc_end] + rcs):
        s_x[COFF - d] = plane
    kx = q_x[COFF - 4] + q_x[COFF - 3]
    for s in range(-3, 1):
        k = at(q_x, kc, s, 0, inward, COFF)
        before, kx = kx, k + at(q_x, kc, s + 1, 0, inward, COFF)
        if s < 0:
            cy_x[COFF + s], cz_x[COFF + s], diag = faces_yz(k, 2)
            diag = diag + before + kx
        else:
            diag = cinv[inward(0)] + before
        scale = inverse(k, diag, 0.8)
        cinv_x[COFF + s] = scale
        e0_x[COFF + s] = s_x[COFF + s] * scale


def sweep(first, last, e_at, q_at, rc_at, cy_at, cz_at, cinv_at, emit):
    flux_x = (q_at(first - 1) + q_at(first)) * (e_at(first - 1) - e_at(first))
    for c in range(first, last + 1):
        e = e_at(c)
        out = flux_yz(e, cy_at(c), cz_at(c), 2) - flux_x
        flux_x = (q_at(c) + q_at(c + 1)) * (e - e_at(c + 1))
        emit(c, e + cinv_at(c) * (rc_at(c) - (out + flux_x)))


def mid_kernel(
    u_ref, k_ref, r_ref, rc_ref, kc_ref,
    ky_ref, kz_ref, inv_ref, d0_ref, r1_ref, d1_ref, sum_ref, smooth_ref,
    cy_ref, cz_ref, cinv_ref, e0_ref,
):
    core = lax.rem(lax.axis_index("pencil"), 2)
    kx = None
    for p in range(NX):
        k = k_ref[p]
        ky_ref[p], kz_ref[p], diag = faces_yz(k)
        if kx is not None:
            diag = diag + kx
        if p < NX - 1:
            kx = k + k_ref[p + 1]
            diag = diag + kx
        if 0 < p < NX - 1:
            inv = inverse(k, diag)
            inv_ref[p] = inv
            d0_ref[p] = r_ref[p] * inv * (1.0 / THETA)
        else:
            inv_ref[p] = diag
    flux_x = (k_ref[1] + k_ref[2]) * (d0_ref[1] - d0_ref[2])
    for p in range(2, NX - 2):
        d0 = d0_ref[p]
        out = flux_yz(d0, ky_ref[p], kz_ref[p]) - flux_x
        flux_x = (k_ref[p] + k_ref[p + 1]) * (d0 - d0_ref[p + 1])
        r1 = r_ref[p] - (out + flux_x)
        d1 = step_d1(r1, d0, inv_ref[p])
        r1_ref[p], d1_ref[p] = r1, d1
        sum_ref[p] = u_ref[place(core, p, NX)] + main(d0) + main(d1)
    flux_x = main((k_ref[2] + k_ref[3]) * (d1_ref[2] - d1_ref[3]))
    for p in range(3, NX - 3):
        d1 = d1_ref[p]
        out = main(flux_yz(d1, ky_ref[p], kz_ref[p])) - flux_x
        flux_x = main((k_ref[p] + k_ref[p + 1]) * (d1 - d1_ref[p + 1]))
        smooth_ref[p] = main(r1_ref[p]) - (out + flux_x)
    kx = None
    for c in range(CX):
        k = kc_ref[c]
        cy_ref[c], cz_ref[c], diag = faces_yz(k, 2)
        if kx is not None:
            diag = diag + kx
        if c < CX - 1:
            kx = k + kc_ref[c + 1]
            diag = diag + kx
        if 0 < c < CX - 1:
            inv = inverse(k, diag, 0.8)
            cinv_ref[c] = inv
            e0_ref[c] = rc_ref[c] * inv
        else:
            cinv_ref[c] = diag


def chip_kernel(
    u_ref, uo_ref, ko_ref, k_ref, r_ref, rc_ref, kc_ref,
    ky_ref, kz_ref, inv_ref, d0_ref, r1_ref, d1_ref,
    cy_ref, cz_ref, cinv_ref, e0_ref, msg_ref,
    sum_ref, smooth_ref, q_x, s_x, cinv_x, e1_x, e2_x,
    k_x, r_x, ky_x, kz_x, inv_x, d0_x, d1_x, cy_x, cz_x, e0_x, tmp_ref,
):
    core = lax.rem(lax.axis_index("pencil"), 2)
    opened = open_message(msg_ref, uo_ref[1], ko_ref[1], r_ref[NX - 1], rc_ref[CX - 1], tmp_ref)

    def emit(s, rest, step):
        smooth_ref[s] = rest
        if s < 2:
            sum_ref[s] = u_ref[place(core, NX - 1 - s, NX)] + step

    fine_side(
        opened, lambda s: NX - 1 - s,
        (k_ref, r_ref, ky_ref, kz_ref, inv_ref, d0_ref, r1_ref, d1_ref),
        (k_x, r_x, ky_x, kz_x, inv_x, d0_x, d1_x), emit,
    )

    def inward(s):
        return CX - 1 - s

    coarse_side(opened, inward, kc_ref, cinv_ref, (q_x, s_x, cy_x, cz_x, cinv_x, e0_x))

    def pick(near, own, first):
        return lambda s: at(near, own, s, first, inward, COFF)

    rest = (
        pick(q_x, kc_ref, 0), pick(s_x, rc_ref, 1), pick(cy_x, cy_ref, 0), pick(cz_x, cz_ref, 0),
        pick(cinv_x, cinv_ref, 1),
    )

    def keep(ref):
        def store(s, e):
            ref[COFF + s] = e

        return store

    sweep(-2, 1, pick(e0_x, e0_ref, 1), *rest, keep(e1_x))
    sweep(-1, 0, lambda s: e1_x[COFF + s], *rest, keep(e2_x))


def final_kernel(
    u_ref, uo_ref, ko_ref, k_ref, r_ref, rc_ref, kc_ref,
    ky_ref, kz_ref, inv_ref, d0_ref, r1_ref, d1_ref, sum_ref, smooth_ref,
    cy_ref, cz_ref, cinv_ref, e0_ref,
    sum_c, smooth_c, q_c, s_c, cinv_c, e1_c, e2_c, msg_ref,
    new_hbm, smooth_hbm,
    k_x, r_x, ky_x, kz_x, inv_x, d0_x, d1_x, q_x, s_x, cy_x, cz_x, cinv_x, e0_x, e1_x, e2_x,
    tmp_ref, lift_ref, new_ref, out_ref, new_sem, smooth_sem,
):
    core = lax.rem(lax.axis_index("pencil"), 2)
    copies = []

    def put(src, dst, sem, p):
        copies.append(pltpu.make_async_copy(src, dst.at[place(core, p, NX)], sem.at[p]))
        copies[-1].start()

    for p in range(3, NX):
        put(smooth_ref.at[p] if p < NX - 3 else smooth_c.at[NX - 1 - p], smooth_hbm, smooth_sem, p)
    opened = open_message(msg_ref, uo_ref[0], ko_ref[0], r_ref[0], rc_ref[0], tmp_ref)

    def emit(p, rest, step):
        out_ref[p] = rest
        put(out_ref.at[p], smooth_hbm, smooth_sem, p)
        if p < 2:
            new_ref[p] = u_ref[place(core, p, NX)] + step

    fine_side(
        opened, lambda s: s,
        (k_ref, r_ref, ky_ref, kz_ref, inv_ref, d0_ref, r1_ref, d1_ref),
        (k_x, r_x, ky_x, kz_x, inv_x, d0_x, d1_x), emit,
    )
    coarse_side(opened, lambda s: s, kc_ref, cinv_ref, (q_x, s_x, cy_x, cz_x, cinv_x, e0_x))

    def pick(near, own, first, far=None, beyond=CX):
        def read(c):
            if c < first:
                return near[COFF + c]
            return own[c] if c < beyond else far[COFF + CX - 1 - c]

        return read

    rest = (
        pick(q_x, kc_ref, 0, q_c), pick(s_x, rc_ref, 1, s_c, 3), pick(cy_x, cy_ref, 0),
        pick(cz_x, cz_ref, 0), pick(cinv_x, cinv_ref, 1, cinv_c, 3),
    )

    def keep(ref):
        def store(c, e):
            ref[COFF + c] = e

        return store

    def lift(c, e):
        cols = []
        for t in range(NZ // 128):
            part = e[:CY, t * 128 : (t + 1) * 128]
            tile = lift_ref.at[2 * c + t]
            tile[pl.ds(0, CY, stride=2), :] = part
            tile[pl.ds(1, CY, stride=2), :] = part
            cols.append(tile[...])
        lifted = jnp.concatenate(cols, axis=1)
        for p in (2 * c, 2 * c + 1):
            if p < 2:
                done = new_ref[p]
            else:
                done = sum_ref[p] if p < NX - 2 else sum_c[NX - 1 - p]
            new_ref[p] = done + lifted
            put(new_ref.at[p], new_hbm, new_sem, p)

    sweep(-2, 1, pick(e0_x, e0_ref, 1), *rest, keep(e1_x))
    sweep(-1, 2, pick(e1_x, None, 2, e1_c, 2), *rest, keep(e2_x))
    sweep(0, 3, pick(e2_x, None, 3, e2_c, 3), *rest, lift)
    for copy in copies:
        copy.wait()


def call(kernel, outs, specs, scratch, bytes_accessed, flops):
    spaces = {"s": pltpu.SMEM, "v": pltpu.VMEM, "h": pltpu.HBM}
    return pl.pallas_call(
        kernel,
        out_shape=[jax.ShapeDtypeStruct(tuple(s), f32) for s in outs],
        in_specs=[pl.BlockSpec(memory_space=spaces[s]) for s in specs],
        out_specs=[
            pl.BlockSpec(memory_space=pl.ANY if isinstance(s, list) else pltpu.VMEM) for s in outs
        ],
        scratch_shapes=[pltpu.VMEM(s, f32) if isinstance(s, tuple) else s for s in scratch],
        compiler_params=pltpu.CompilerParams(vmem_limit_bytes=16 << 20),
        cost_estimate=pl.CostEstimate(flops=flops, bytes_accessed=bytes_accessed, transcendentals=0),
    )


def shifted(cells, axis, by):
    count = lax.axis_size(axis)
    return lax.ppermute(cells, axis, [(i, i + by) for i in range(count) if 0 <= i + by < count])


def swapped(cells, axis, first):
    count = lax.axis_size(axis)
    pairs = []
    for i in range(first, count - 1, 2):
        pairs += [(i, i + 1), (i + 1, i)]
    return lax.ppermute(cells, axis, pairs)


def on_device(right_side, conductivity, guess):
    own = (NX, NY, NZ)
    dma = pltpu.SemaphoreType.DMA
    u, k, f, upward, downward, ends = call(
        pack_kernel,
        [own, own, own, (GROUPS, H, NZ), (GROUPS, H, NZ), [16, NY, 256]],
        "hhh", [(2, NY, 256), dma((6,)), dma((6,))], 1 << 20, 1 << 18,
    )(*(pltpu.with_memory_space_constraint(a, pltpu.HBM) for a in (guess, conductivity, right_side)))
    upward = shifted(upward, "coarse", 1)
    downward = shifted(downward, "coarse", -1)
    ends = lax.all_to_all(ends, ("gz", "coarse"), 0, 0)

    def fine(n):
        return (n, RF, ZE)

    def coarse(n):
        return (n, CE, ZE)

    message = (X_GROUPS + 2, 8, NZ)
    edges = (ZE // 128, RE, 128)
    rows = [(NX, NY, ZE)] * 3 + [(CX, CY, ZE)] * 2
    tiles = [(NX, 2 * H, 128)] * 3
    parts = call(
        own_kernel, rows + tiles, "v" * 4, [(NX, ZE // 128, NY, 128)], 3 << 20, 1 << 22,
    )(u, k, f, ends)
    uo, ko, k_in, r_in, rc, kc, chip, link = call(
        edge_kernel,
        [(2, RE, ZE), (2, RE, ZE), fine(NX), fine(NX), coarse(CX), coarse(CX), message, message],
        "v" * 10, [(NX, ZE // 128, NY, 128)], 3 << 20, 1 << 22,
    )(*parts, upward, downward)
    chip = swapped(chip, "pencil", 0)
    link = swapped(link, "pencil", 1)
    *fine_own, sums, smooth, cy, cz, cinv, e0 = call(
        mid_kernel, [fine(NX)] * 6 + [own, own] + [coarse(CX)] * 4, "v" * 5, [],
        4 << 20, 1 << 22,
    )(u, k_in, r_in, rc, kc)
    half = call(
        chip_kernel,
        [(2, NY, NZ), (3, NY, NZ)] + [coarse(5)] * 3 + [coarse(6)] * 2, "v" * 18,
        [fine(3), fine(5)] + [fine(5)] * 5 + [coarse(5)] * 3 + [edges], 4 << 20, 1 << 22,
    )(u, uo, ko, k_in, r_in, rc, kc, *fine_own, cy, cz, cinv, e0, chip)
    return tuple(
        call(
            final_kernel, [list(own), list(own)], "v" * 27,
            [fine(3), fine(5)] + [fine(5)] * 5 + [coarse(5)] * 6 + [coarse(6), coarse(7)]
            + [edges, (NX, NY, 128), own, (3, NY, NZ), dma((NX,)), dma((NX,))],
            4 << 20, 1 << 22,
        )(u, uo, ko, k_in, r_in, rc, kc, *fine_own, sums, smooth, cy, cz, cinv, e0, *half, link)
    )


def solution(mesh):
    spec = P("pencil", "coarse", "gz")
    return jax.shard_map(
        on_device,
        mesh=mesh,
        in_specs=(spec, spec, spec),
        out_specs=(spec, spec),
        check_vma=False,
    )
```

```python
import jax
import jax.numpy as jnp
from jax import lax
from jax.experimental import pallas as pl
from jax.experimental.pallas import tpu as pltpu
from jax.sharding import PartitionSpec as P


THETA = 1.1
DELTA = 0.8
SIGMA = THETA / DELTA
RHO0 = 1.0 / SIGMA
RHO1 = 1.0 / (2.0 * SIGMA - RHO0)

NX, NY, NZ = 8, 16, 256
H = 8
RE = NY + 2 * H
RF = NY + H
ZE = NZ + 128
CX, CY = NX // 2, NY // 2
CE = RE // 2
GROUPS = 3 * NX
f32 = jnp.float32


def up(v, axis, by=1):
    return pltpu.roll(v, v.shape[axis] - by, axis)


def down(v, axis, by=1):
    return pltpu.roll(v, by, axis)


def lanes(shape):
    return lax.broadcasted_iota(jnp.int32, shape, len(shape) - 1)


def pack_kernel(
    u_hbm, k_hbm, f_hbm,
    u_ref, k_ref, f_ref, one_ref, two_ref, z_hbm,
    end_ref, own_sem, end_sem,
):
    gz, cy = lax.axis_index("gz"), lax.axis_index("coarse")
    core = lax.rem(lax.axis_index("pencil"), 2)
    fields = (u_ref, k_ref, f_ref)
    copies = []
    for i, (far, near) in enumerate(zip((u_hbm, k_hbm, f_hbm), fields)):
        for half in range(2):
            at = pl.ds(half * NX // 2, NX // 2)
            copies.append(pltpu.make_async_copy(far.at[at], near.at[at], own_sem.at[2 * i + half]))
            copies[-1].start()
    for copy in copies:
        copy.wait()
    group = lanes((NY, 128)) // H
    sends = []
    for side, (first, start, to_z) in enumerate(((NZ - 128, H, 1), (0, 0, 3))):
        for t in range(2):
            tile = jnp.zeros((NY, 128), f32)
            for q in range(16):
                g = t * 16 + q
                if g < GROUPS:
                    cells = fields[g // NX][g % NX, :, first : first + 128]
                    shift = (H * q + start) % 128
                    moved = pltpu.roll(cells, shift, 1) if shift else cells
                    tile = jnp.where(group == q, moved, tile)
            end_ref[side, :, t * 128 : (t + 1) * 128] = tile
        z = lax.rem(gz + to_z, 4) * 4
        end = end_ref.at[side]
        for j, (src, dst) in enumerate((
            (end, z_hbm.at[z + cy]),
            (end.at[pl.ds(NY - H, H)], z_hbm.at[z + lax.rem(cy + 1, 4), pl.ds(0, H)]),
            (end.at[pl.ds(0, H)], z_hbm.at[z + lax.rem(cy + 3, 4), pl.ds(0, H)]),
        )):
            sends.append(pltpu.make_async_copy(src, dst, end_sem.at[3 * side + j]))
            sends[-1].start()
    for ref, start in ((one_ref, (1 - core) * (NY - H)), (two_ref, core * (NY - H))):
        rows = pl.ds(pl.multiple_of(start, 8), H)
        for i, field in enumerate(fields):
            for p in range(NX):
                ref[i * NX + p] = field[p, rows, :]
    for copy in sends:
        copy.wait()


def lane_pairs(plane, even):
    return plane + jnp.where(even, up(plane, 1), down(plane, 1))


def restrict_plane(plane, scratch_ref, even, scale):
    rows, cols = plane.shape[0], []
    for t in range(ZE // 128):
        tile = scratch_ref.at[t]
        tile[:rows] = plane[:, t * 128 : (t + 1) * 128]
        cols.append(tile[pl.ds(0, rows // 2, stride=2), :] + tile[pl.ds(1, rows // 2, stride=2), :])
    return scale * lane_pairs(jnp.concatenate(cols, axis=1), even)


def place(core, p, count):
    return core * (count - 1) + (1 - 2 * core) * p


def inner_rows(plane):
    row = lax.broadcasted_iota(jnp.int32, (H, ZE), 0)
    return jnp.concatenate(
        [plane[:NY], jnp.where(row < H // 2, plane[NY : NY + H], plane[NY + H :])], axis=0
    )


X_U, X_K, X_K2, X_K3, X_R1, X_R2, X_C = 0, 4, 8, 11, 13, 16, 18
X_GROUPS = X_C + 3 * 2 + 1
X_TAIL = X_GROUPS


def send_rows(ref, tails, first, plane):
    for j in range(plane.shape[0] // 8):
        rows = plane[j * 8 : (j + 1) * 8]
        ref[first + j] = rows[:, :NZ]
        tails[first + j] = rows[:, NZ:]


def send_tails(ref, tails):
    lane = lanes((8, 128)) // 16
    for half in range(4):
        tile = jnp.zeros((8, 128), f32)
        for j in range(8):
            g = half * 8 + j
            if g < X_GROUPS:
                shift = (16 * j + 8) % 128
                tile = jnp.where(lane == j, pltpu.roll(tails[g], shift, 1), tile)
        ref[X_TAIL + half // 2, :, (half % 2) * 128 : (half % 2) * 128 + 128] = tile


def received_rows(ref, first, groups):
    rows = []
    for g in range(first, first + groups):
        half, j = divmod(g, 8)
        tile = ref[X_TAIL + half // 2, :, (half % 2) * 128 : (half % 2) * 128 + 128]
        rows.append(jnp.concatenate([ref[g], pltpu.roll(tile, (120 - 16 * j) % 128, 1)], axis=1) if (120 - 16 * j) % 128 else jnp.concatenate([ref[g], tile], axis=1))
    return jnp.concatenate(rows, axis=0)


def own_kernel(
    u_ref, k_ref, f_ref, z_ref,
    uo_ref, ko_ref, ro_ref, rc_ref, kc_ref, zu_ref, zk_ref, zf_ref,
    tmp_ref,
):
    gz, cy = lax.axis_index("gz"), lax.axis_index("coarse")
    lane = lanes((RE, 128))
    sides = []
    for from_z, inside in ((3, gz > 0), (1, gz < 3)):
        z = lax.rem(gz + from_z, 4) * 4
        rows = [
            z_ref[z + cy],
            jnp.where(cy < 3, z_ref[z + lax.rem(cy + 1, 4), :H], 0.0),
            jnp.where(cy > 0, z_ref[z + lax.rem(cy + 3, 4), :H], 0.0),
        ]
        sides.append(jnp.where(inside, jnp.concatenate(rows, axis=0), 0.0))

    def extended(i, p, own, halo):
        t, q = divmod(i * NX + p, 16)
        before, after = (side[:, t * 128 : t * 128 + 128] for side in sides)
        if (120 - H * q) % 128:
            before = pltpu.roll(before, (120 - H * q) % 128, 1)
        if q:
            after = pltpu.roll(after, 128 - H * q, 1)
        beyond = jnp.where(lane < H, after, jnp.where(lane >= 120, before, 0.0))
        cells = own[p]
        if i == 1:
            beyond, cells = 0.5 * beyond, 0.5 * cells
        halo[p] = beyond[NY:]
        return jnp.concatenate([cells, beyond[:NY]], axis=1)

    even = lanes((CY, ZE)) % 2 == 0
    inner = lax.broadcasted_iota(jnp.int32, (NY, ZE), 0) < NY - 1
    flux_x = r_pair = k_pair = None
    u, k = extended(0, 0, u_ref, zu_ref), extended(1, 0, k_ref, zk_ref)
    for p in range(NX):
        uo_ref[p], ko_ref[p] = u, k
        flux = (k + up(k, 1)) * (u - up(u, 1))
        out = flux - down(flux, 1)
        flux = jnp.where(inner, (k + up(k, 0)) * (u - up(u, 0)), 0.0)
        out = out + (flux - down(flux, 0))
        if flux_x is not None:
            out = out - flux_x
        r, k_now = extended(2, p, f_ref, zf_ref), k
        if p < NX - 1:
            un, kn = extended(0, p + 1, u_ref, zu_ref), extended(1, p + 1, k_ref, zk_ref)
            flux_x = (k + kn) * (u - un)
            out = out + flux_x
            u, k = un, kn
        r = r - out
        ro_ref[p] = r
        if p % 2 == 0:
            r_pair, k_pair = r, k_now
        else:
            rc_ref[p // 2] = restrict_plane(r_pair + r, tmp_ref.at[p - 1], even, 0.125)
            kc_ref[p // 2] = restrict_plane(k_pair + k_now, tmp_ref.at[p], even, 0.03125)


def edge_kernel(
    u_ref, k_ref, r_ref, rcl_ref, kcl_ref, zu_ref, zk_ref, zf_ref, one_ref, two_ref,
    uo_ref, ko_ref, k_in_ref, r_in_ref, rc_ref, kc_ref, chip_ref, link_ref,
    tmp_ref,
):
    core = lax.rem(lax.axis_index("pencil"), 2)
    row = lax.broadcasted_iota(jnp.int32, (H, ZE), 0)
    even = lanes((CY, ZE)) % 2 == 0

    def halo(i, p, beyond):
        g = i * NX + p
        scale = (lambda v: 0.5 * v) if i == 1 else (lambda v: v)
        one, two = scale(one_ref[g]), scale(two_ref[g])
        after, before = jnp.where(core == 1, one, two), jnp.where(core == 1, two, one)
        cells = jnp.concatenate([after, before], axis=0)
        return jnp.concatenate([cells, beyond[p]], axis=1)

    flux_x = r_pair = k_pair = d_pair = None
    u, k = halo(0, 0, zu_ref), halo(1, 0, zk_ref)
    for p in range(NX):
        own_u, own_k, own_r = u_ref[p], k_ref[p], r_ref[p]
        flux = (k + up(k, 1)) * (u - up(u, 1))
        out = flux - down(flux, 1)
        kl, ul, kv, uv = k[:H], u[:H], k[H:], u[H:]
        low = (down(own_k[H:], 0) + kl) * (down(own_u[H:], 0) - ul)
        high = (kv + up(own_k[:H], 0)) * (uv - up(own_u[:H], 0))
        flux = (kl + up(kl, 0)) * (ul - up(ul, 0))
        below = flux - jnp.where(row == 0, low, down(flux, 0))
        flux = jnp.where(row == H - 1, high, (kv + up(kv, 0)) * (uv - up(uv, 0)))
        out = out + jnp.concatenate([below, flux - down(flux, 0)], axis=0)
        first = jnp.where(row == 0, down(high, 0), 0.0)
        last = jnp.where(row == H - 1, up(low, 0), 0.0)
        if flux_x is not None:
            out = out - flux_x
        r, k_now, u_now = halo(2, p, zf_ref), k, u
        if p < NX - 1:
            un, kn = halo(0, p + 1, zu_ref), halo(1, p + 1, zk_ref)
            flux_x = (k + kn) * (u - un)
            out = out + flux_x
            u, k = un, kn
        r = r - out
        q = place(core, p, NX)
        near = row < H // 2
        r_in_ref[q] = jnp.concatenate(
            [own_r[:H] + first, own_r[H:] - last, jnp.where(near, r[:H], r[H:])], axis=0
        )
        k_in_ref[q] = jnp.concatenate([own_k, jnp.where(near, k_now[:H], k_now[H:])], axis=0)
        if p in (0, NX - 1):
            end = place(core, p // (NX - 1), 2)
            uo_ref[end] = jnp.concatenate([own_u, u_now], axis=0)
            ko_ref[end] = jnp.concatenate([own_k, k_now], axis=0)
        if p % 2 == 0:
            r_pair, k_pair, d_pair = r, k_now, first - last
        else:
            c = place(core, p // 2, CX)
            rc_ref[c] = jnp.concatenate([
                rcl_ref[p // 2] + 0.125 * lane_pairs(d_pair + (first - last), even),
                restrict_plane(r_pair + r, tmp_ref.at[p - 1], even, 0.125),
            ], axis=0)
            kc_ref[c] = jnp.concatenate(
                [kcl_ref[p // 2], restrict_plane(k_pair + k_now, tmp_ref.at[p], even, 0.03125)], axis=0
            )
    even_c = lanes((CE, ZE)) % 2 == 0
    for i, ref in enumerate((link_ref, chip_ref)):
        at, step, c = i * (NX - 1), 1 - 2 * i, i * (CX - 1)
        tails = {}
        send_rows(ref, tails, X_U, uo_ref[i])
        send_rows(ref, tails, X_K, ko_ref[i])
        send_rows(ref, tails, X_K2, k_in_ref[at + step])
        send_rows(ref, tails, X_K3, k_in_ref[at + 2 * step, :NY])
        send_rows(ref, tails, X_R1, r_in_ref[at])
        send_rows(ref, tails, X_R2, r_in_ref[at + step, :NY])
        for d in range(CX):
            both = jnp.where(even_c, rc_ref[c + d * step], kc_ref[c + d * step])
            send_rows(ref, tails, X_C + 2 * d, both if d < 3 else both[:CY])
        send_tails(ref, tails)


def faces_yz(k, by=1):
    ky, kz = k + up(k, 0), k + up(k, 1, by)
    return ky, kz, (ky + down(ky, 0)) + (kz + down(kz, 1, by))


def flux_yz(v, ky, kz, by=1):
    flux = kz * (v - up(v, 1, by))
    out = flux - down(flux, 1, by)
    flux = ky * (v - up(v, 0))
    return out + (flux - down(flux, 0))


def inverse(k, diag, scale=1.0):
    return jnp.where(k > 0.0, scale / diag, 0.0)


def step_d1(r1, d0, inv):
    return (RHO1 * RHO0) * d0 + (2.0 * RHO1 / DELTA) * (r1 * inv)


def main(v):
    return v[:NY, :NZ]


def open_message(msg, u_end, k_end, r_end, rc_end, tmp_ref):
    even_c = lanes((CE, ZE)) % 2 == 0
    none = jnp.zeros((RF - NY, ZE), f32)
    un, kn = received_rows(msg, X_U, 4), received_rows(msg, X_K, 4)
    flux = (k_end + kn) * (u_end - un)
    inner = inner_rows(flux)
    coarse = restrict_plane(flux, tmp_ref, even_c, 0.125)
    ks = [inner_rows(kn), received_rows(msg, X_K2, 3)]
    ks.append(jnp.concatenate([received_rows(msg, X_K3, 2), none], axis=0))
    rs = [received_rows(msg, X_R1, 3) + inner]
    rs.append(jnp.concatenate([received_rows(msg, X_R2, 2), none], axis=0))
    kcs, rcs = [], []
    for d in range(CX):
        if d < 3:
            both = received_rows(msg, X_C + 2 * d, 2)
            rc = jnp.where(even_c, both, down(both, 1))
            rcs.append(rc + coarse if d == 0 else rc)
        else:
            both = jnp.concatenate([received_rows(msg, X_C + 2 * d, 1), none], axis=0)
        kcs.append(jnp.where(even_c, up(both, 1), both))
    return r_end - inner, ks, rs, rc_end - coarse, kcs, rcs


OFF, COFF = 3, 4


def at(near, own, s, first, inward, off=OFF):
    return own[inward(s)] if s >= first else near[off + s]


def fine_side(opened, inward, own, near, emit):
    r_end, ks, rs = opened[:3]
    k, r, ky, kz, inv, d0, r1, d1 = own
    k_x, r_x, ky_x, kz_x, inv_x, d0_x, d1_x = near
    for d, plane in enumerate(ks):
        k_x[OFF - 1 - d] = plane
    for d, plane in enumerate([r_end] + rs):
        r_x[OFF - d] = plane

    def k_at(s):
        return at(k_x, k, s, 0, inward)

    def d0_at(s):
        return at(d0_x, d0, s, 1, inward)

    def d1_at(s):
        return at(d1_x, d1, s, 2, inward)

    def faces_at(s):
        return at(ky_x, ky, s, 0, inward), at(kz_x, kz, s, 0, inward)

    kx = k_at(-3) + k_at(-2)
    for s in range(-2, 1):
        kv = k_at(s)
        before, kx = kx, kv + k_at(s + 1)
        if s < 0:
            ky_x[OFF + s], kz_x[OFF + s], diag = faces_yz(kv)
            diag = diag + before + kx
        else:
            diag = inv[inward(0)] + before
        scale = inverse(kv, diag)
        inv_x[OFF + s] = scale
        d0_x[OFF + s] = r_x[OFF + s] * scale * (1.0 / THETA)
    flux_x = (k_at(-2) + k_at(-1)) * (d0_at(-2) - d0_at(-1))
    for s in range(-1, 2):
        v = d0_at(s)
        out = flux_yz(v, *faces_at(s)) - flux_x
        flux_x = (k_at(s) + k_at(s + 1)) * (v - d0_at(s + 1))
        rv = at(r_x, r, s, 1, inward) - (out + flux_x)
        r_x[OFF + s] = rv
        d1_x[OFF + s] = step_d1(rv, v, at(inv_x, inv, s, 1, inward))
    flux_x = main((k_at(-1) + k_at(0)) * (d1_at(-1) - d1_at(0)))
    for s in range(3):
        v = d1_at(s)
        out = main(flux_yz(v, *faces_at(s))) - flux_x
        flux_x = main((k_at(s) + k_at(s + 1)) * (v - d1_at(s + 1)))
        rest = main(at(r_x, r1, s, 2, inward)) - (out + flux_x)
        emit(s, rest, main(d0_at(s)) + main(v) if s < 2 else None)


def coarse_side(opened, inward, kc, cinv, near):
    rc_end, kcs, rcs = opened[3:]
    q_x, s_x, cy_x, cz_x, cinv_x, e0_x = near
    for d, plane in enumerate(kcs):
        q_x[COFF - 1 - d] = plane
    for d, plane in enumerate([rc_end] + rcs):
        s_x[COFF - d] = plane
    kx = q_x[COFF - 4] + q_x[COFF - 3]
    for s in range(-3, 1):
        k = at(q_x, kc, s, 0, inward, COFF)
        before, kx = kx, k + at(q_x, kc, s + 1, 0, inward, COFF)
        if s < 0:
            cy_x[COFF + s], cz_x[COFF + s], diag = faces_yz(k, 2)
            diag = diag + before + kx
        else:
            diag = cinv[inward(0)] + before
        scale = inverse(k, diag, 0.8)
        cinv_x[COFF + s] = scale
        e0_x[COFF + s] = s_x[COFF + s] * scale


def sweep(first, last, e_at, q_at, rc_at, cy_at, cz_at, cinv_at, emit):
    flux_x = (q_at(first - 1) + q_at(first)) * (e_at(first - 1) - e_at(first))
    for c in range(first, last + 1):
        e = e_at(c)
        out = flux_yz(e, cy_at(c), cz_at(c), 2) - flux_x
        flux_x = (q_at(c) + q_at(c + 1)) * (e - e_at(c + 1))
        emit(c, e + cinv_at(c) * (rc_at(c) - (out + flux_x)))


def mid_kernel(
    u_ref, k_ref, r_ref, rc_ref, kc_ref,
    ky_ref, kz_ref, inv_ref, d0_ref, r1_ref, d1_ref, sum_ref, smooth_ref,
    cy_ref, cz_ref, cinv_ref, e0_ref,
):
    core = lax.rem(lax.axis_index("pencil"), 2)
    kx = None
    for p in range(NX):
        k = k_ref[p]
        ky_ref[p], kz_ref[p], diag = faces_yz(k)
        if kx is not None:
            diag = diag + kx
        if p < NX - 1:
            kx = k + k_ref[p + 1]
            diag = diag + kx
        if 0 < p < NX - 1:
            inv = inverse(k, diag)
            inv_ref[p] = inv
            d0_ref[p] = r_ref[p] * inv * (1.0 / THETA)
        else:
            inv_ref[p] = diag
    flux_x = (k_ref[1] + k_ref[2]) * (d0_ref[1] - d0_ref[2])
    for p in range(2, NX - 2):
        d0 = d0_ref[p]
        out = flux_yz(d0, ky_ref[p], kz_ref[p]) - flux_x
        flux_x = (k_ref[p] + k_ref[p + 1]) * (d0 - d0_ref[p + 1])
        r1 = r_ref[p] - (out + flux_x)
        d1 = step_d1(r1, d0, inv_ref[p])
        r1_ref[p], d1_ref[p] = r1, d1
        sum_ref[p] = u_ref[place(core, p, NX)] + main(d0) + main(d1)
    flux_x = main((k_ref[2] + k_ref[3]) * (d1_ref[2] - d1_ref[3]))
    for p in range(3, NX - 3):
        d1 = d1_ref[p]
        out = main(flux_yz(d1, ky_ref[p], kz_ref[p])) - flux_x
        flux_x = main((k_ref[p] + k_ref[p + 1]) * (d1 - d1_ref[p + 1]))
        smooth_ref[p] = main(r1_ref[p]) - (out + flux_x)
    kx = None
    for c in range(CX):
        k = kc_ref[c]
        cy_ref[c], cz_ref[c], diag = faces_yz(k, 2)
        if kx is not None:
            diag = diag + kx
        if c < CX - 1:
            kx = k + kc_ref[c + 1]
            diag = diag + kx
        if 0 < c < CX - 1:
            inv = inverse(k, diag, 0.8)
            cinv_ref[c] = inv
            e0_ref[c] = rc_ref[c] * inv
        else:
            cinv_ref[c] = diag


def chip_kernel(
    u_ref, uo_ref, ko_ref, k_ref, r_ref, rc_ref, kc_ref,
    ky_ref, kz_ref, inv_ref, d0_ref, r1_ref, d1_ref,
    cy_ref, cz_ref, cinv_ref, e0_ref, msg_ref,
    sum_ref, smooth_ref, q_x, s_x, cinv_x, e1_x, e2_x,
    k_x, r_x, ky_x, kz_x, inv_x, d0_x, d1_x, cy_x, cz_x, e0_x, tmp_ref,
):
    core = lax.rem(lax.axis_index("pencil"), 2)
    opened = open_message(msg_ref, uo_ref[1], ko_ref[1], r_ref[NX - 1], rc_ref[CX - 1], tmp_ref)

    def emit(s, rest, step):
        smooth_ref[s] = rest
        if s < 2:
            sum_ref[s] = u_ref[place(core, NX - 1 - s, NX)] + step

    fine_side(
        opened, lambda s: NX - 1 - s,
        (k_ref, r_ref, ky_ref, kz_ref, inv_ref, d0_ref, r1_ref, d1_ref),
        (k_x, r_x, ky_x, kz_x, inv_x, d0_x, d1_x), emit,
    )

    def inward(s):
        return CX - 1 - s

    coarse_side(opened, inward, kc_ref, cinv_ref, (q_x, s_x, cy_x, cz_x, cinv_x, e0_x))

    def pick(near, own, first):
        return lambda s: at(near, own, s, first, inward, COFF)

    rest = (
        pick(q_x, kc_ref, 0), pick(s_x, rc_ref, 1), pick(cy_x, cy_ref, 0), pick(cz_x, cz_ref, 0),
        pick(cinv_x, cinv_ref, 1),
    )

    def keep(ref):
        def store(s, e):
            ref[COFF + s] = e

        return store

    sweep(-2, 1, pick(e0_x, e0_ref, 1), *rest, keep(e1_x))
    sweep(-1, 0, lambda s: e1_x[COFF + s], *rest, keep(e2_x))


def final_kernel(
    u_ref, uo_ref, ko_ref, k_ref, r_ref, rc_ref, kc_ref,
    ky_ref, kz_ref, inv_ref, d0_ref, r1_ref, d1_ref, sum_ref, smooth_ref,
    cy_ref, cz_ref, cinv_ref, e0_ref,
    sum_c, smooth_c, q_c, s_c, cinv_c, e1_c, e2_c, msg_ref,
    new_hbm, smooth_hbm,
    k_x, r_x, ky_x, kz_x, inv_x, d0_x, d1_x, q_x, s_x, cy_x, cz_x, cinv_x, e0_x, e1_x, e2_x,
    tmp_ref, lift_ref, new_ref, out_ref, new_sem, smooth_sem,
):
    core = lax.rem(lax.axis_index("pencil"), 2)
    copies = []

    def put(src, dst, sem, p):
        copies.append(pltpu.make_async_copy(src, dst.at[place(core, p, NX)], sem.at[p]))
        copies[-1].start()

    for p in range(3, NX):
        put(smooth_ref.at[p] if p < NX - 3 else smooth_c.at[NX - 1 - p], smooth_hbm, smooth_sem, p)
    opened = open_message(msg_ref, uo_ref[0], ko_ref[0], r_ref[0], rc_ref[0], tmp_ref)

    def emit(p, rest, step):
        out_ref[p] = rest
        put(out_ref.at[p], smooth_hbm, smooth_sem, p)
        if p < 2:
            new_ref[p] = u_ref[place(core, p, NX)] + step

    fine_side(
        opened, lambda s: s,
        (k_ref, r_ref, ky_ref, kz_ref, inv_ref, d0_ref, r1_ref, d1_ref),
        (k_x, r_x, ky_x, kz_x, inv_x, d0_x, d1_x), emit,
    )
    coarse_side(opened, lambda s: s, kc_ref, cinv_ref, (q_x, s_x, cy_x, cz_x, cinv_x, e0_x))

    def pick(near, own, first, far=None, beyond=CX):
        def read(c):
            if c < first:
                return near[COFF + c]
            return own[c] if c < beyond else far[COFF + CX - 1 - c]

        return read

    rest = (
        pick(q_x, kc_ref, 0, q_c), pick(s_x, rc_ref, 1, s_c, 3), pick(cy_x, cy_ref, 0),
        pick(cz_x, cz_ref, 0), pick(cinv_x, cinv_ref, 1, cinv_c, 3),
    )

    def keep(ref):
        def store(c, e):
            ref[COFF + c] = e

        return store

    def lift(c, e):
        cols = []
        for t in range(NZ // 128):
            part = e[:CY, t * 128 : (t + 1) * 128]
            tile = lift_ref.at[2 * c + t]
            tile[pl.ds(0, CY, stride=2), :] = part
            tile[pl.ds(1, CY, stride=2), :] = part
            cols.append(tile[...])
        lifted = jnp.concatenate(cols, axis=1)
        for p in (2 * c, 2 * c + 1):
            if p < 2:
                done = new_ref[p]
            else:
                done = sum_ref[p] if p < NX - 2 else sum_c[NX - 1 - p]
            new_ref[p] = done + lifted
            put(new_ref.at[p], new_hbm, new_sem, p)

    sweep(-2, 1, pick(e0_x, e0_ref, 1), *rest, keep(e1_x))
    sweep(-1, 2, pick(e1_x, None, 2, e1_c, 2), *rest, keep(e2_x))
    sweep(0, 3, pick(e2_x, None, 3, e2_c, 3), *rest, lift)
    for copy in copies:
        copy.wait()


def call(kernel, outs, specs, scratch, bytes_accessed, flops):
    spaces = {"s": pltpu.SMEM, "v": pltpu.VMEM, "h": pltpu.HBM}
    return pl.pallas_call(
        kernel,
        out_shape=[jax.ShapeDtypeStruct(tuple(s), f32) for s in outs],
        in_specs=[pl.BlockSpec(memory_space=spaces[s]) for s in specs],
        out_specs=[
            pl.BlockSpec(memory_space=pl.ANY if isinstance(s, list) else pltpu.VMEM) for s in outs
        ],
        scratch_shapes=[pltpu.VMEM(s, f32) if isinstance(s, tuple) else s for s in scratch],
        compiler_params=pltpu.CompilerParams(vmem_limit_bytes=16 << 20),
        cost_estimate=pl.CostEstimate(flops=flops, bytes_accessed=bytes_accessed, transcendentals=0),
    )


def parted(cells, by):
    count = lax.axis_size("coarse")
    pairs = []
    for p in range(lax.axis_size("pencil")):
        step = by if p % 2 == 0 else -by
        pairs += [
            (p * count + i, p * count + i + step) for i in range(count) if 0 <= i + step < count
        ]
    return lax.ppermute(cells, ("pencil", "coarse"), pairs)


def swapped(cells, axis, first):
    count = lax.axis_size(axis)
    pairs = []
    for i in range(first, count - 1, 2):
        pairs += [(i, i + 1), (i + 1, i)]
    return lax.ppermute(cells, axis, pairs)


def on_device(right_side, conductivity, guess):
    own = (NX, NY, NZ)
    dma = pltpu.SemaphoreType.DMA
    u, k, f, one, two, ends = call(
        pack_kernel,
        [own, own, own, (GROUPS, H, NZ), (GROUPS, H, NZ), [16, NY, 256]],
        "hhh", [(2, NY, 256), dma((6,)), dma((6,))], 1 << 20, 1 << 18,
    )(*(pltpu.with_memory_space_constraint(a, pltpu.HBM) for a in (guess, conductivity, right_side)))
    one = parted(one, 1)
    two = parted(two, -1)
    ends = lax.all_to_all(ends, ("gz", "coarse"), 0, 0)

    def fine(n):
        return (n, RF, ZE)

    def coarse(n):
        return (n, CE, ZE)

    message = (X_GROUPS + 2, 8, NZ)
    edges = (ZE // 128, RE, 128)
    rows = [(NX, NY, ZE)] * 3 + [(CX, CY, ZE)] * 2
    tiles = [(NX, 2 * H, 128)] * 3
    parts = call(
        own_kernel, rows + tiles, "v" * 4, [(NX, ZE // 128, NY, 128)], 3 << 20, 1 << 22,
    )(u, k, f, ends)
    uo, ko, k_in, r_in, rc, kc, chip, link = call(
        edge_kernel,
        [(2, RE, ZE), (2, RE, ZE), fine(NX), fine(NX), coarse(CX), coarse(CX), message, message],
        "v" * 10, [(NX, ZE // 128, NY, 128)], 3 << 20, 1 << 22,
    )(*parts, one, two)
    chip = swapped(chip, "pencil", 0)
    link = swapped(link, "pencil", 1)
    *fine_own, sums, smooth, cy, cz, cinv, e0 = call(
        mid_kernel, [fine(NX)] * 6 + [own, own] + [coarse(CX)] * 4, "v" * 5, [],
        4 << 20, 1 << 22,
    )(u, k_in, r_in, rc, kc)
    half = call(
        chip_kernel,
        [(2, NY, NZ), (3, NY, NZ)] + [coarse(5)] * 3 + [coarse(6)] * 2, "v" * 18,
        [fine(3), fine(5)] + [fine(5)] * 5 + [coarse(5)] * 3 + [edges], 4 << 20, 1 << 22,
    )(u, uo, ko, k_in, r_in, rc, kc, *fine_own, cy, cz, cinv, e0, chip)
    return tuple(
        call(
            final_kernel, [list(own), list(own)], "v" * 27,
            [fine(3), fine(5)] + [fine(5)] * 5 + [coarse(5)] * 6 + [coarse(6), coarse(7)]
            + [edges, (NX, NY, 128), own, (3, NY, NZ), dma((NX,)), dma((NX,))],
            4 << 20, 1 << 22,
        )(u, uo, ko, k_in, r_in, rc, kc, *fine_own, sums, smooth, cy, cz, cinv, e0, *half, link)
    )


def solution(mesh):
    spec = P("pencil", "coarse", "gz")
    return jax.shard_map(
        on_device,
        mesh=mesh,
        in_specs=(spec, spec, spec),
        out_specs=(spec, spec),
        check_vma=False,
    )
```

```python
import jax
import jax.numpy as jnp
from jax import lax
from jax.experimental import pallas as pl
from jax.experimental.pallas import tpu as pltpu
from jax.sharding import PartitionSpec as P


THETA = 1.1
DELTA = 0.8
SIGMA = THETA / DELTA
RHO0 = 1.0 / SIGMA
RHO1 = 1.0 / (2.0 * SIGMA - RHO0)

NX, NY, NZ = 8, 16, 256
H = 8
RE = NY + 2 * H
RF = NY + H
ZE = NZ + 128
CX, CY = NX // 2, NY // 2
CE = RE // 2
GROUPS = 3 * NX - 2
f32 = jnp.float32


def up(v, axis, by=1):
    return pltpu.roll(v, v.shape[axis] - by, axis)


def down(v, axis, by=1):
    return pltpu.roll(v, by, axis)


def lanes(shape):
    return lax.broadcasted_iota(jnp.int32, shape, len(shape) - 1)


def pack_kernel(
    u_hbm, k_hbm, f_hbm,
    u_ref, k_ref, f_ref, one_ref, two_ref, z_hbm,
    end_ref, own_sem, end_sem,
):
    gz, cy = lax.axis_index("gz"), lax.axis_index("coarse")
    core = lax.rem(lax.axis_index("pencil"), 2)
    fields = (u_ref, k_ref, f_ref)
    copies = []
    for i, (far, near) in enumerate(zip((u_hbm, k_hbm, f_hbm), fields)):
        for half in range(2):
            at = pl.ds(half * NX // 2, NX // 2)
            copies.append(pltpu.make_async_copy(far.at[at], near.at[at], own_sem.at[2 * i + half]))
            copies[-1].start()
    for copy in copies:
        copy.wait()
    group = lanes((H, 128)) // H
    sends = []
    for side, (first, start, to_z) in enumerate(((NZ - 128, H, 1), (0, 0, 3))):
        for tile in range(3):
            packed = jnp.zeros((H, 128), f32)
            for q in range(16):
                if tile == 1:
                    field, rows = f_ref, (0, NY - H)[q // NX]
                else:
                    field, rows = fields[q // NX], (0, NY - H)[tile // 2]
                cells = field[q % NX, rows : rows + H, first : first + 128]
                shift = (H * q + start) % 128
                moved = pltpu.roll(cells, shift, 1) if shift else cells
                packed = jnp.where(group == q, moved, packed)
            end_ref[side, tile] = packed
        z = lax.rem(gz + to_z, 4) * 4
        end = end_ref.at[side]
        for j, (src, dst) in enumerate((
            (end, z_hbm.at[z + cy]),
            (end.at[pl.ds(1, 2)], z_hbm.at[z + lax.rem(cy + 1, 4), pl.ds(1, 2)]),
            (end.at[pl.ds(0, 2)], z_hbm.at[z + lax.rem(cy + 3, 4), pl.ds(0, 2)]),
        )):
            sends.append(pltpu.make_async_copy(src, dst, end_sem.at[3 * side + j]))
            sends[-1].start()
    for ref, start in ((one_ref, (1 - core) * (NY - H)), (two_ref, core * (NY - H))):
        rows = pl.ds(pl.multiple_of(start, 8), H)
        for i, field in enumerate(fields):
            for p in range(NX if i < 2 else 0):
                ref[i * NX + p] = field[p, rows, :]
        row = lax.broadcasted_iota(jnp.int32, (H, NZ), 0)
        spare = (row + jnp.where(start > 0, 0, 2)) % H < 2
        for p in range(NX - 2):
            moved = pltpu.roll(f_ref[NX - 2 + p // 3, rows, :], 6 - 2 * (p % 3), 0)
            ref[2 * NX + p] = jnp.where(spare, moved, f_ref[p, rows, :])
    for copy in sends:
        copy.wait()


def lane_pairs(plane, even):
    return plane + jnp.where(even, up(plane, 1), down(plane, 1))


def restrict_plane(plane, scratch_ref, even, scale):
    rows, cols = plane.shape[0], []
    for t in range(ZE // 128):
        tile = scratch_ref.at[t]
        tile[:rows] = plane[:, t * 128 : (t + 1) * 128]
        cols.append(tile[pl.ds(0, rows // 2, stride=2), :] + tile[pl.ds(1, rows // 2, stride=2), :])
    return scale * lane_pairs(jnp.concatenate(cols, axis=1), even)


def place(core, p, count):
    return core * (count - 1) + (1 - 2 * core) * p


def inner_rows(plane):
    row = lax.broadcasted_iota(jnp.int32, (H, ZE), 0)
    return jnp.concatenate(
        [plane[:NY], jnp.where(row < H // 2, plane[NY : NY + H], plane[NY + H :])], axis=0
    )


X_U, X_K, X_K2, X_K3, X_R1, X_R2, X_C = 0, 4, 8, 11, 13, 16, 18
X_GROUPS = X_C + 3 * 2 + 1
X_TAIL = X_GROUPS


def send_rows(ref, tails, first, plane):
    for j in range(plane.shape[0] // 8):
        rows = plane[j * 8 : (j + 1) * 8]
        ref[first + j] = rows[:, :NZ]
        tails[first + j] = rows[:, NZ:]


def send_tails(ref, tails):
    lane = lanes((8, 128)) // 16
    for half in range(4):
        tile = jnp.zeros((8, 128), f32)
        for j in range(8):
            g = half * 8 + j
            if g < X_GROUPS:
                shift = (16 * j + 8) % 128
                tile = jnp.where(lane == j, pltpu.roll(tails[g], shift, 1), tile)
        ref[X_TAIL + half // 2, :, (half % 2) * 128 : (half % 2) * 128 + 128] = tile


def received_rows(ref, first, groups):
    rows = []
    for g in range(first, first + groups):
        half, j = divmod(g, 8)
        tile = ref[X_TAIL + half // 2, :, (half % 2) * 128 : (half % 2) * 128 + 128]
        rows.append(jnp.concatenate([ref[g], pltpu.roll(tile, (120 - 16 * j) % 128, 1)], axis=1) if (120 - 16 * j) % 128 else jnp.concatenate([ref[g], tile], axis=1))
    return jnp.concatenate(rows, axis=0)


def own_kernel(
    u_ref, k_ref, f_ref, z_ref,
    uo_ref, ko_ref, ro_ref, rc_ref, kc_ref, zu_ref, zk_ref, zf_ref,
    tmp_ref,
):
    gz, cy = lax.axis_index("gz"), lax.axis_index("coarse")
    lane = lanes((RE, 128))
    sides = []
    for from_z, inside in ((3, gz > 0), (1, gz < 3)):
        z = lax.rem(gz + from_z, 4) * 4
        same, after, before = (z + lax.rem(cy + d, 4) for d in (0, 1, 3))
        uk = [
            z_ref[same, 0], z_ref[same, 2],
            jnp.where(cy < 3, z_ref[after, 0], 0.0), jnp.where(cy > 0, z_ref[before, 2], 0.0),
        ]
        f = [
            z_ref[same, 1], pltpu.roll(z_ref[same, 1], 64, 1),
            jnp.where(cy < 3, z_ref[after, 1], 0.0),
            jnp.where(cy > 0, pltpu.roll(z_ref[before, 1], 64, 1), 0.0),
        ]
        sides.append(tuple(jnp.where(inside, jnp.concatenate(v, axis=0), 0.0) for v in (uk, f)))

    def extended(i, p, own, halo):
        t, q = divmod(i * NX + p, 16)
        before, after = (side[t] for side in sides)
        if (120 - H * q) % 128:
            before = pltpu.roll(before, (120 - H * q) % 128, 1)
        if q:
            after = pltpu.roll(after, 128 - H * q, 1)
        beyond = jnp.where(lane < H, after, jnp.where(lane >= 120, before, 0.0))
        cells = own[p]
        if i == 1:
            beyond, cells = 0.5 * beyond, 0.5 * cells
        halo[p] = beyond[NY:]
        return jnp.concatenate([cells, beyond[:NY]], axis=1)

    even = lanes((CY, ZE)) % 2 == 0
    inner = lax.broadcasted_iota(jnp.int32, (NY, ZE), 0) < NY - 1
    flux_x = r_pair = k_pair = None
    u, k = extended(0, 0, u_ref, zu_ref), extended(1, 0, k_ref, zk_ref)
    for p in range(NX):
        uo_ref[p], ko_ref[p] = u, k
        flux = (k + up(k, 1)) * (u - up(u, 1))
        out = flux - down(flux, 1)
        flux = jnp.where(inner, (k + up(k, 0)) * (u - up(u, 0)), 0.0)
        out = out + (flux - down(flux, 0))
        if flux_x is not None:
            out = out - flux_x
        r, k_now = extended(2, p, f_ref, zf_ref), k
        if p < NX - 1:
            un, kn = extended(0, p + 1, u_ref, zu_ref), extended(1, p + 1, k_ref, zk_ref)
            flux_x = (k + kn) * (u - un)
            out = out + flux_x
            u, k = un, kn
        r = r - out
        ro_ref[p] = r
        if p % 2 == 0:
            r_pair, k_pair = r, k_now
        else:
            rc_ref[p // 2] = restrict_plane(r_pair + r, tmp_ref.at[p - 1], even, 0.125)
            kc_ref[p // 2] = restrict_plane(k_pair + k_now, tmp_ref.at[p], even, 0.03125)


def edge_kernel(
    u_ref, k_ref, r_ref, rcl_ref, kcl_ref, zu_ref, zk_ref, zf_ref, one_ref, two_ref,
    uo_ref, ko_ref, k_in_ref, r_in_ref, rc_ref, kc_ref, chip_ref, link_ref,
    tmp_ref,
):
    core = lax.rem(lax.axis_index("pencil"), 2)
    row = lax.broadcasted_iota(jnp.int32, (H, ZE), 0)
    even = lanes((CY, ZE)) % 2 == 0

    pair = lax.broadcasted_iota(jnp.int32, (H, NZ), 0) // 2

    def tiles(g):
        one, two = one_ref[g], two_ref[g]
        return jnp.where(core == 1, one, two), jnp.where(core == 1, two, one)

    def halo(i, p, beyond):
        if i < 2 or p < NX - 2:
            after, before = tiles(i * NX + p)
        else:
            after = before = jnp.zeros((H, NZ), f32)
            for j in range(3):
                a, b = tiles(2 * NX + 3 * (p - NX + 2) + j)
                after = jnp.where(pair == j, pltpu.roll(a, 2 + 2 * j, 0), after)
                before = jnp.where(pair == j + 1, pltpu.roll(b, 2 + 2 * j, 0), before)
        cells = jnp.concatenate([after, before], axis=0)
        return jnp.concatenate([0.5 * cells if i == 1 else cells, beyond[p]], axis=1)

    flux_x = r_pair = k_pair = d_pair = None
    u, k = halo(0, 0, zu_ref), halo(1, 0, zk_ref)
    for p in range(NX):
        own_u, own_k, own_r = u_ref[p], k_ref[p], r_ref[p]
        flux = (k + up(k, 1)) * (u - up(u, 1))
        out = flux - down(flux, 1)
        kl, ul, kv, uv = k[:H], u[:H], k[H:], u[H:]
        low = (down(own_k[H:], 0) + kl) * (down(own_u[H:], 0) - ul)
        high = (kv + up(own_k[:H], 0)) * (uv - up(own_u[:H], 0))
        flux = (kl + up(kl, 0)) * (ul - up(ul, 0))
        below = flux - jnp.where(row == 0, low, down(flux, 0))
        flux = jnp.where(row == H - 1, high, (kv + up(kv, 0)) * (uv - up(uv, 0)))
        out = out + jnp.concatenate([below, flux - down(flux, 0)], axis=0)
        first = jnp.where(row == 0, down(high, 0), 0.0)
        last = jnp.where(row == H - 1, up(low, 0), 0.0)
        if flux_x is not None:
            out = out - flux_x
        r, k_now, u_now = halo(2, p, zf_ref), k, u
        if p < NX - 1:
            un, kn = halo(0, p + 1, zu_ref), halo(1, p + 1, zk_ref)
            flux_x = (k + kn) * (u - un)
            out = out + flux_x
            u, k = un, kn
        r = r - out
        q = place(core, p, NX)
        near = row < H // 2
        r_in_ref[q] = jnp.concatenate(
            [own_r[:H] + first, own_r[H:] - last, jnp.where(near, r[:H], r[H:])], axis=0
        )
        k_in_ref[q] = jnp.concatenate([own_k, jnp.where(near, k_now[:H], k_now[H:])], axis=0)
        if p in (0, NX - 1):
            end = place(core, p // (NX - 1), 2)
            uo_ref[end] = jnp.concatenate([own_u, u_now], axis=0)
            ko_ref[end] = jnp.concatenate([own_k, k_now], axis=0)
        if p % 2 == 0:
            r_pair, k_pair, d_pair = r, k_now, first - last
        else:
            c = place(core, p // 2, CX)
            rc_ref[c] = jnp.concatenate([
                rcl_ref[p // 2] + 0.125 * lane_pairs(d_pair + (first - last), even),
                restrict_plane(r_pair + r, tmp_ref.at[p - 1], even, 0.125),
            ], axis=0)
            kc_ref[c] = jnp.concatenate(
                [kcl_ref[p // 2], restrict_plane(k_pair + k_now, tmp_ref.at[p], even, 0.03125)], axis=0
            )
    even_c = lanes((CE, ZE)) % 2 == 0
    for i, ref in enumerate((link_ref, chip_ref)):
        at, step, c = i * (NX - 1), 1 - 2 * i, i * (CX - 1)
        tails = {}
        send_rows(ref, tails, X_U, uo_ref[i])
        send_rows(ref, tails, X_K, ko_ref[i])
        send_rows(ref, tails, X_K2, k_in_ref[at + step])
        send_rows(ref, tails, X_K3, k_in_ref[at + 2 * step, :NY])
        send_rows(ref, tails, X_R1, r_in_ref[at])
        send_rows(ref, tails, X_R2, r_in_ref[at + step, :NY])
        for d in range(CX):
            both = jnp.where(even_c, rc_ref[c + d * step], kc_ref[c + d * step])
            send_rows(ref, tails, X_C + 2 * d, both if d < 3 else both[:CY])
        send_tails(ref, tails)


def faces_yz(k, by=1):
    ky, kz = k + up(k, 0), k + up(k, 1, by)
    return ky, kz, (ky + down(ky, 0)) + (kz + down(kz, 1, by))


def flux_yz(v, ky, kz, by=1):
    flux = kz * (v - up(v, 1, by))
    out = flux - down(flux, 1, by)
    flux = ky * (v - up(v, 0))
    return out + (flux - down(flux, 0))


def inverse(k, diag, scale=1.0):
    return jnp.where(k > 0.0, scale / diag, 0.0)


def step_d1(r1, d0, inv):
    return (RHO1 * RHO0) * d0 + (2.0 * RHO1 / DELTA) * (r1 * inv)


def main(v):
    return v[:NY, :NZ]


def open_message(msg, u_end, k_end, r_end, rc_end, tmp_ref):
    even_c = lanes((CE, ZE)) % 2 == 0
    none = jnp.zeros((RF - NY, ZE), f32)
    un, kn = received_rows(msg, X_U, 4), received_rows(msg, X_K, 4)
    flux = (k_end + kn) * (u_end - un)
    inner = inner_rows(flux)
    coarse = restrict_plane(flux, tmp_ref, even_c, 0.125)
    ks = [inner_rows(kn), received_rows(msg, X_K2, 3)]
    ks.append(jnp.concatenate([received_rows(msg, X_K3, 2), none], axis=0))
    rs = [received_rows(msg, X_R1, 3) + inner]
    rs.append(jnp.concatenate([received_rows(msg, X_R2, 2), none], axis=0))
    kcs, rcs = [], []
    for d in range(CX):
        if d < 3:
            both = received_rows(msg, X_C + 2 * d, 2)
            rc = jnp.where(even_c, both, down(both, 1))
            rcs.append(rc + coarse if d == 0 else rc)
        else:
            both = jnp.concatenate([received_rows(msg, X_C + 2 * d, 1), none], axis=0)
        kcs.append(jnp.where(even_c, up(both, 1), both))
    return r_end - inner, ks, rs, rc_end - coarse, kcs, rcs


OFF, COFF = 3, 4


def at(near, own, s, first, inward, off=OFF):
    return own[inward(s)] if s >= first else near[off + s]


def fine_side(opened, inward, own, near, emit):
    r_end, ks, rs = opened[:3]
    k, r, ky, kz, inv, d0, r1, d1 = own
    k_x, r_x, ky_x, kz_x, inv_x, d0_x, d1_x = near
    for d, plane in enumerate(ks):
        k_x[OFF - 1 - d] = plane
    for d, plane in enumerate([r_end] + rs):
        r_x[OFF - d] = plane

    def k_at(s):
        return at(k_x, k, s, 0, inward)

    def d0_at(s):
        return at(d0_x, d0, s, 1, inward)

    def d1_at(s):
        return at(d1_x, d1, s, 2, inward)

    def faces_at(s):
        return at(ky_x, ky, s, 0, inward), at(kz_x, kz, s, 0, inward)

    kx = k_at(-3) + k_at(-2)
    for s in range(-2, 1):
        kv = k_at(s)
        before, kx = kx, kv + k_at(s + 1)
        if s < 0:
            ky_x[OFF + s], kz_x[OFF + s], diag = faces_yz(kv)
            diag = diag + before + kx
        else:
            diag = inv[inward(0)] + before
        scale = inverse(kv, diag)
        inv_x[OFF + s] = scale
        d0_x[OFF + s] = r_x[OFF + s] * scale * (1.0 / THETA)
    flux_x = (k_at(-2) + k_at(-1)) * (d0_at(-2) - d0_at(-1))
    for s in range(-1, 2):
        v = d0_at(s)
        out = flux_yz(v, *faces_at(s)) - flux_x
        flux_x = (k_at(s) + k_at(s + 1)) * (v - d0_at(s + 1))
        rv = at(r_x, r, s, 1, inward) - (out + flux_x)
        r_x[OFF + s] = rv
        d1_x[OFF + s] = step_d1(rv, v, at(inv_x, inv, s, 1, inward))
    flux_x = main((k_at(-1) + k_at(0)) * (d1_at(-1) - d1_at(0)))
    for s in range(3):
        v = d1_at(s)
        out = main(flux_yz(v, *faces_at(s))) - flux_x
        flux_x = main((k_at(s) + k_at(s + 1)) * (v - d1_at(s + 1)))
        rest = main(at(r_x, r1, s, 2, inward)) - (out + flux_x)
        emit(s, rest, main(d0_at(s)) + main(v) if s < 2 else None)


def coarse_side(opened, inward, kc, cinv, near):
    rc_end, kcs, rcs = opened[3:]
    q_x, s_x, cy_x, cz_x, cinv_x, e0_x = near
    for d, plane in enumerate(kcs):
        q_x[COFF - 1 - d] = plane
    for d, plane in enumerate([rc_end] + rcs):
        s_x[COFF - d] = plane
    kx = q_x[COFF - 4] + q_x[COFF - 3]
    for s in range(-3, 1):
        k = at(q_x, kc, s, 0, inward, COFF)
        before, kx = kx, k + at(q_x, kc, s + 1, 0, inward, COFF)
        if s < 0:
            cy_x[COFF + s], cz_x[COFF + s], diag = faces_yz(k, 2)
            diag = diag + before + kx
        else:
            diag = cinv[inward(0)] + before
        scale = inverse(k, diag, 0.8)
        cinv_x[COFF + s] = scale
        e0_x[COFF + s] = s_x[COFF + s] * scale


def sweep(first, last, e_at, q_at, rc_at, cy_at, cz_at, cinv_at, emit):
    flux_x = (q_at(first - 1) + q_at(first)) * (e_at(first - 1) - e_at(first))
    for c in range(first, last + 1):
        e = e_at(c)
        out = flux_yz(e, cy_at(c), cz_at(c), 2) - flux_x
        flux_x = (q_at(c) + q_at(c + 1)) * (e - e_at(c + 1))
        emit(c, e + cinv_at(c) * (rc_at(c) - (out + flux_x)))


def mid_kernel(
    u_ref, k_ref, r_ref, rc_ref, kc_ref,
    ky_ref, kz_ref, inv_ref, d0_ref, r1_ref, d1_ref, sum_ref, smooth_ref,
    cy_ref, cz_ref, cinv_ref, e0_ref,
):
    core = lax.rem(lax.axis_index("pencil"), 2)
    kx = None
    for p in range(NX):
        k = k_ref[p]
        ky_ref[p], kz_ref[p], diag = faces_yz(k)
        if kx is not None:
            diag = diag + kx
        if p < NX - 1:
            kx = k + k_ref[p + 1]
            diag = diag + kx
        if 0 < p < NX - 1:
            inv = inverse(k, diag)
            inv_ref[p] = inv
            d0_ref[p] = r_ref[p] * inv * (1.0 / THETA)
        else:
            inv_ref[p] = diag
    flux_x = (k_ref[1] + k_ref[2]) * (d0_ref[1] - d0_ref[2])
    for p in range(2, NX - 2):
        d0 = d0_ref[p]
        out = flux_yz(d0, ky_ref[p], kz_ref[p]) - flux_x
        flux_x = (k_ref[p] + k_ref[p + 1]) * (d0 - d0_ref[p + 1])
        r1 = r_ref[p] - (out + flux_x)
        d1 = step_d1(r1, d0, inv_ref[p])
        r1_ref[p], d1_ref[p] = r1, d1
        sum_ref[p] = u_ref[place(core, p, NX)] + main(d0) + main(d1)
    flux_x = main((k_ref[2] + k_ref[3]) * (d1_ref[2] - d1_ref[3]))
    for p in range(3, NX - 3):
        d1 = d1_ref[p]
        out = main(flux_yz(d1, ky_ref[p], kz_ref[p])) - flux_x
        flux_x = main((k_ref[p] + k_ref[p + 1]) * (d1 - d1_ref[p + 1]))
        smooth_ref[p] = main(r1_ref[p]) - (out + flux_x)
    kx = None
    for c in range(CX):
        k = kc_ref[c]
        cy_ref[c], cz_ref[c], diag = faces_yz(k, 2)
        if kx is not None:
            diag = diag + kx
        if c < CX - 1:
            kx = k + kc_ref[c + 1]
            diag = diag + kx
        if 0 < c < CX - 1:
            inv = inverse(k, diag, 0.8)
            cinv_ref[c] = inv
            e0_ref[c] = rc_ref[c] * inv
        else:
            cinv_ref[c] = diag


def chip_kernel(
    u_ref, uo_ref, ko_ref, k_ref, r_ref, rc_ref, kc_ref,
    ky_ref, kz_ref, inv_ref, d0_ref, r1_ref, d1_ref,
    cy_ref, cz_ref, cinv_ref, e0_ref, msg_ref,
    sum_ref, smooth_ref, q_x, s_x, cinv_x, e1_x, e2_x,
    k_x, r_x, ky_x, kz_x, inv_x, d0_x, d1_x, cy_x, cz_x, e0_x, tmp_ref,
):
    core = lax.rem(lax.axis_index("pencil"), 2)
    opened = open_message(msg_ref, uo_ref[1], ko_ref[1], r_ref[NX - 1], rc_ref[CX - 1], tmp_ref)

    def emit(s, rest, step):
        smooth_ref[s] = rest
        if s < 2:
            sum_ref[s] = u_ref[place(core, NX - 1 - s, NX)] + step

    fine_side(
        opened, lambda s: NX - 1 - s,
        (k_ref, r_ref, ky_ref, kz_ref, inv_ref, d0_ref, r1_ref, d1_ref),
        (k_x, r_x, ky_x, kz_x, inv_x, d0_x, d1_x), emit,
    )

    def inward(s):
        return CX - 1 - s

    coarse_side(opened, inward, kc_ref, cinv_ref, (q_x, s_x, cy_x, cz_x, cinv_x, e0_x))

    def pick(near, own, first):
        return lambda s: at(near, own, s, first, inward, COFF)

    rest = (
        pick(q_x, kc_ref, 0), pick(s_x, rc_ref, 1), pick(cy_x, cy_ref, 0), pick(cz_x, cz_ref, 0),
        pick(cinv_x, cinv_ref, 1),
    )

    def keep(ref):
        def store(s, e):
            ref[COFF + s] = e

        return store

    sweep(-2, 1, pick(e0_x, e0_ref, 1), *rest, keep(e1_x))
    sweep(-1, 0, lambda s: e1_x[COFF + s], *rest, keep(e2_x))


def final_kernel(
    u_ref, uo_ref, ko_ref, k_ref, r_ref, rc_ref, kc_ref,
    ky_ref, kz_ref, inv_ref, d0_ref, r1_ref, d1_ref, sum_ref, smooth_ref,
    cy_ref, cz_ref, cinv_ref, e0_ref,
    sum_c, smooth_c, q_c, s_c, cinv_c, e1_c, e2_c, msg_ref,
    new_hbm, smooth_hbm,
    k_x, r_x, ky_x, kz_x, inv_x, d0_x, d1_x, q_x, s_x, cy_x, cz_x, cinv_x, e0_x, e1_x, e2_x,
    tmp_ref, lift_ref, new_ref, out_ref, new_sem, smooth_sem,
):
    core = lax.rem(lax.axis_index("pencil"), 2)
    copies = []

    def put(src, dst, sem, p):
        copies.append(pltpu.make_async_copy(src, dst.at[place(core, p, NX)], sem.at[p]))
        copies[-1].start()

    for p in range(3, NX):
        put(smooth_ref.at[p] if p < NX - 3 else smooth_c.at[NX - 1 - p], smooth_hbm, smooth_sem, p)
    opened = open_message(msg_ref, uo_ref[0], ko_ref[0], r_ref[0], rc_ref[0], tmp_ref)

    def emit(p, rest, step):
        out_ref[p] = rest
        put(out_ref.at[p], smooth_hbm, smooth_sem, p)
        if p < 2:
            new_ref[p] = u_ref[place(core, p, NX)] + step

    fine_side(
        opened, lambda s: s,
        (k_ref, r_ref, ky_ref, kz_ref, inv_ref, d0_ref, r1_ref, d1_ref),
        (k_x, r_x, ky_x, kz_x, inv_x, d0_x, d1_x), emit,
    )
    coarse_side(opened, lambda s: s, kc_ref, cinv_ref, (q_x, s_x, cy_x, cz_x, cinv_x, e0_x))

    def pick(near, own, first, far=None, beyond=CX):
        def read(c):
            if c < first:
                return near[COFF + c]
            return own[c] if c < beyond else far[COFF + CX - 1 - c]

        return read

    rest = (
        pick(q_x, kc_ref, 0, q_c), pick(s_x, rc_ref, 1, s_c, 3), pick(cy_x, cy_ref, 0),
        pick(cz_x, cz_ref, 0), pick(cinv_x, cinv_ref, 1, cinv_c, 3),
    )

    def keep(ref):
        def store(c, e):
            ref[COFF + c] = e

        return store

    def lift(c, e):
        cols = []
        for t in range(NZ // 128):
            part = e[:CY, t * 128 : (t + 1) * 128]
            tile = lift_ref.at[2 * c + t]
            tile[pl.ds(0, CY, stride=2), :] = part
            tile[pl.ds(1, CY, stride=2), :] = part
            cols.append(tile[...])
        lifted = jnp.concatenate(cols, axis=1)
        for p in (2 * c, 2 * c + 1):
            if p < 2:
                done = new_ref[p]
            else:
                done = sum_ref[p] if p < NX - 2 else sum_c[NX - 1 - p]
            new_ref[p] = done + lifted
            put(new_ref.at[p], new_hbm, new_sem, p)

    sweep(-2, 1, pick(e0_x, e0_ref, 1), *rest, keep(e1_x))
    sweep(-1, 2, pick(e1_x, None, 2, e1_c, 2), *rest, keep(e2_x))
    sweep(0, 3, pick(e2_x, None, 3, e2_c, 3), *rest, lift)
    for copy in copies:
        copy.wait()


def call(kernel, outs, specs, scratch, bytes_accessed, flops):
    spaces = {"s": pltpu.SMEM, "v": pltpu.VMEM, "h": pltpu.HBM}
    return pl.pallas_call(
        kernel,
        out_shape=[jax.ShapeDtypeStruct(tuple(s), f32) for s in outs],
        in_specs=[pl.BlockSpec(memory_space=spaces[s]) for s in specs],
        out_specs=[
            pl.BlockSpec(memory_space=pl.ANY if isinstance(s, list) else pltpu.VMEM) for s in outs
        ],
        scratch_shapes=[pltpu.VMEM(s, f32) if isinstance(s, tuple) else s for s in scratch],
        compiler_params=pltpu.CompilerParams(vmem_limit_bytes=16 << 20),
        cost_estimate=pl.CostEstimate(flops=flops, bytes_accessed=bytes_accessed, transcendentals=0),
    )


def parted(cells, by):
    count = lax.axis_size("coarse")
    pairs = []
    for p in range(lax.axis_size("pencil")):
        step = by if p % 2 == 0 else -by
        pairs += [
            (p * count + i, p * count + i + step) for i in range(count) if 0 <= i + step < count
        ]
    return lax.ppermute(cells, ("pencil", "coarse"), pairs)


def swapped(cells, axis, first):
    count = lax.axis_size(axis)
    pairs = []
    for i in range(first, count - 1, 2):
        pairs += [(i, i + 1), (i + 1, i)]
    return lax.ppermute(cells, axis, pairs)


def on_device(right_side, conductivity, guess):
    own = (NX, NY, NZ)
    dma = pltpu.SemaphoreType.DMA
    u, k, f, one, two, ends = call(
        pack_kernel,
        [own, own, own, (GROUPS, H, NZ), (GROUPS, H, NZ), [16, 3, H, 128]],
        "hhh", [(2, 3, H, 128), dma((6,)), dma((6,))], 1 << 20, 1 << 18,
    )(*(pltpu.with_memory_space_constraint(a, pltpu.HBM) for a in (guess, conductivity, right_side)))
    one = parted(one, 1)
    two = parted(two, -1)
    ends = lax.all_to_all(ends, ("gz", "coarse"), 0, 0)

    def fine(n):
        return (n, RF, ZE)

    def coarse(n):
        return (n, CE, ZE)

    message = (X_GROUPS + 2, 8, NZ)
    edges = (ZE // 128, RE, 128)
    rows = [(NX, NY, ZE)] * 3 + [(CX, CY, ZE)] * 2
    tiles = [(NX, 2 * H, 128)] * 3
    parts = call(
        own_kernel, rows + tiles, "v" * 4, [(NX, ZE // 128, NY, 128)], 3 << 20, 1 << 22,
    )(u, k, f, ends)
    uo, ko, k_in, r_in, rc, kc, chip, link = call(
        edge_kernel,
        [(2, RE, ZE), (2, RE, ZE), fine(NX), fine(NX), coarse(CX), coarse(CX), message, message],
        "v" * 10, [(NX, ZE // 128, NY, 128)], 3 << 20, 1 << 22,
    )(*parts, one, two)
    chip = swapped(chip, "pencil", 0)
    link = swapped(link, "pencil", 1)
    *fine_own, sums, smooth, cy, cz, cinv, e0 = call(
        mid_kernel, [fine(NX)] * 6 + [own, own] + [coarse(CX)] * 4, "v" * 5, [],
        4 << 20, 1 << 22,
    )(u, k_in, r_in, rc, kc)
    half = call(
        chip_kernel,
        [(2, NY, NZ), (3, NY, NZ)] + [coarse(5)] * 3 + [coarse(6)] * 2, "v" * 18,
        [fine(3), fine(5)] + [fine(5)] * 5 + [coarse(5)] * 3 + [edges], 4 << 20, 1 << 22,
    )(u, uo, ko, k_in, r_in, rc, kc, *fine_own, cy, cz, cinv, e0, chip)
    return tuple(
        call(
            final_kernel, [list(own), list(own)], "v" * 27,
            [fine(3), fine(5)] + [fine(5)] * 5 + [coarse(5)] * 6 + [coarse(6), coarse(7)]
            + [edges, (NX, NY, 128), own, (3, NY, NZ), dma((NX,)), dma((NX,))],
            4 << 20, 1 << 22,
        )(u, uo, ko, k_in, r_in, rc, kc, *fine_own, sums, smooth, cy, cz, cinv, e0, *half, link)
    )


def solution(mesh):
    spec = P("pencil", "coarse", "gz")
    return jax.shard_map(
        on_device,
        mesh=mesh,
        in_specs=(spec, spec, spec),
        out_specs=(spec, spec),
        check_vma=False,
    )
```

```python
import jax
import jax.numpy as jnp
from jax import lax
from jax.experimental import pallas as pl
from jax.experimental.pallas import tpu as pltpu
from jax.sharding import PartitionSpec as P


THETA = 1.1
DELTA = 0.8
SIGMA = THETA / DELTA
RHO0 = 1.0 / SIGMA
RHO1 = 1.0 / (2.0 * SIGMA - RHO0)

NX, NY, NZ = 8, 16, 256
H = 8
RE = NY + 2 * H
RF = NY + H
ZE = NZ + 128
CX, CY = NX // 2, NY // 2
CE = RE // 2
GROUPS = 3 * NX - 2
f32 = jnp.float32


def up(v, axis, by=1):
    return pltpu.roll(v, v.shape[axis] - by, axis)


def down(v, axis, by=1):
    return pltpu.roll(v, by, axis)


def lanes(shape):
    return lax.broadcasted_iota(jnp.int32, shape, len(shape) - 1)


def pack_kernel(
    u_hbm, k_hbm, f_hbm,
    u_ref, k_ref, f_ref, one_ref, two_ref, z_hbm,
    end_ref, own_sem, end_sem,
):
    gz, cy = lax.axis_index("gz"), lax.axis_index("coarse")
    core = lax.rem(lax.axis_index("pencil"), 2)
    fields = (u_ref, k_ref, f_ref)
    copies = []
    for i, (far, near) in enumerate(zip((u_hbm, k_hbm, f_hbm), fields)):
        for half in range(2):
            at = pl.ds(half * NX // 2, NX // 2)
            copies.append(pltpu.make_async_copy(far.at[at], near.at[at], own_sem.at[2 * i + half]))
            copies[-1].start()
    group = lanes((H, 128)) // H
    sends = []
    faces = ((NZ - 128, H, 1), (0, 0, 3))
    for copy in copies[:4]:
        copy.wait()
    for tile in (0, 2, 1):
        if tile == 1:
            for copy in copies[4:]:
                copy.wait()
        for side, (first, start, to_z) in enumerate(faces):
            packed = jnp.zeros((H, 128), f32)
            for q in range(16):
                if tile == 1:
                    field, rows = f_ref, (0, NY - H)[q // NX]
                else:
                    field, rows = fields[q // NX], (0, NY - H)[tile // 2]
                cells = field[q % NX, rows : rows + H, first : first + 128]
                shift = (H * q + start) % 128
                moved = pltpu.roll(cells, shift, 1) if shift else cells
                packed = jnp.where(group == q, moved, packed)
            end_ref[side, tile] = packed
    for side, (first, start, to_z) in enumerate(faces):
        z = lax.rem(gz + to_z, 4) * 4
        end = end_ref.at[side]
        for j, (src, dst) in enumerate((
            (end, z_hbm.at[z + cy]),
            (end.at[pl.ds(1, 2)], z_hbm.at[z + lax.rem(cy + 1, 4), pl.ds(1, 2)]),
            (end.at[pl.ds(0, 2)], z_hbm.at[z + lax.rem(cy + 3, 4), pl.ds(0, 2)]),
        )):
            sends.append(pltpu.make_async_copy(src, dst, end_sem.at[3 * side + j]))
            sends[-1].start()
    for ref, start in ((one_ref, (1 - core) * (NY - H)), (two_ref, core * (NY - H))):
        rows = pl.ds(pl.multiple_of(start, 8), H)
        for i, field in enumerate(fields):
            for p in range(NX if i < 2 else 0):
                ref[i * NX + p] = field[p, rows, :]
        row = lax.broadcasted_iota(jnp.int32, (H, NZ), 0)
        spare = (row + jnp.where(start > 0, 0, 2)) % H < 2
        for p in range(NX - 2):
            moved = pltpu.roll(f_ref[NX - 2 + p // 3, rows, :], 6 - 2 * (p % 3), 0)
            ref[2 * NX + p] = jnp.where(spare, moved, f_ref[p, rows, :])
    for copy in sends:
        copy.wait()


def lane_pairs(plane, even):
    return plane + jnp.where(even, up(plane, 1), down(plane, 1))


def restrict_plane(plane, scratch_ref, even, scale):
    rows, cols = plane.shape[0], []
    for t in range(ZE // 128):
        tile = scratch_ref.at[t]
        tile[:rows] = plane[:, t * 128 : (t + 1) * 128]
        cols.append(tile[pl.ds(0, rows // 2, stride=2), :] + tile[pl.ds(1, rows // 2, stride=2), :])
    return scale * lane_pairs(jnp.concatenate(cols, axis=1), even)


def place(core, p, count):
    return core * (count - 1) + (1 - 2 * core) * p


def inner_rows(plane):
    row = lax.broadcasted_iota(jnp.int32, (H, ZE), 0)
    return jnp.concatenate(
        [plane[:NY], jnp.where(row < H // 2, plane[NY : NY + H], plane[NY + H :])], axis=0
    )


X_U, X_K, X_K2, X_K3, X_R1, X_R2, X_C = 0, 4, 8, 11, 13, 16, 18
X_GROUPS = X_C + 3 * 2 + 1
X_TAIL = X_GROUPS


def send_rows(ref, tails, first, plane):
    for j in range(plane.shape[0] // 8):
        rows = plane[j * 8 : (j + 1) * 8]
        ref[first + j] = rows[:, :NZ]
        tails[first + j] = rows[:, NZ:]


def send_tails(ref, tails):
    lane = lanes((8, 128)) // 16
    for half in range(4):
        tile = jnp.zeros((8, 128), f32)
        for j in range(8):
            g = half * 8 + j
            if g < X_GROUPS:
                shift = (16 * j + 8) % 128
                tile = jnp.where(lane == j, pltpu.roll(tails[g], shift, 1), tile)
        ref[X_TAIL + half // 2, :, (half % 2) * 128 : (half % 2) * 128 + 128] = tile


def received_rows(ref, first, groups):
    rows = []
    for g in range(first, first + groups):
        half, j = divmod(g, 8)
        tile = ref[X_TAIL + half // 2, :, (half % 2) * 128 : (half % 2) * 128 + 128]
        rows.append(jnp.concatenate([ref[g], pltpu.roll(tile, (120 - 16 * j) % 128, 1)], axis=1) if (120 - 16 * j) % 128 else jnp.concatenate([ref[g], tile], axis=1))
    return jnp.concatenate(rows, axis=0)


def own_kernel(
    u_ref, k_ref, f_ref, z_ref,
    uo_ref, ko_ref, ro_ref, rc_ref, kc_ref, zu_ref, zk_ref, zf_ref,
    tmp_ref,
):
    gz, cy = lax.axis_index("gz"), lax.axis_index("coarse")
    lane = lanes((RE, 128))
    sides = []
    for from_z, inside in ((3, gz > 0), (1, gz < 3)):
        z = lax.rem(gz + from_z, 4) * 4
        same, after, before = (z + lax.rem(cy + d, 4) for d in (0, 1, 3))
        uk = [
            z_ref[same, 0], z_ref[same, 2],
            jnp.where(cy < 3, z_ref[after, 0], 0.0), jnp.where(cy > 0, z_ref[before, 2], 0.0),
        ]
        f = [
            z_ref[same, 1], pltpu.roll(z_ref[same, 1], 64, 1),
            jnp.where(cy < 3, z_ref[after, 1], 0.0),
            jnp.where(cy > 0, pltpu.roll(z_ref[before, 1], 64, 1), 0.0),
        ]
        sides.append(tuple(jnp.where(inside, jnp.concatenate(v, axis=0), 0.0) for v in (uk, f)))

    def extended(i, p, own, halo):
        t, q = divmod(i * NX + p, 16)
        before, after = (side[t] for side in sides)
        if (120 - H * q) % 128:
            before = pltpu.roll(before, (120 - H * q) % 128, 1)
        if q:
            after = pltpu.roll(after, 128 - H * q, 1)
        beyond = jnp.where(lane < H, after, jnp.where(lane >= 120, before, 0.0))
        cells = own[p]
        if i == 1:
            beyond, cells = 0.5 * beyond, 0.5 * cells
        halo[p] = beyond[NY:]
        return jnp.concatenate([cells, beyond[:NY]], axis=1)

    even = lanes((CY, ZE)) % 2 == 0
    inner = lax.broadcasted_iota(jnp.int32, (NY, ZE), 0) < NY - 1
    flux_x = r_pair = k_pair = None
    u, k = extended(0, 0, u_ref, zu_ref), extended(1, 0, k_ref, zk_ref)
    for p in range(NX):
        uo_ref[p], ko_ref[p] = u, k
        flux = (k + up(k, 1)) * (u - up(u, 1))
        out = flux - down(flux, 1)
        flux = jnp.where(inner, (k + up(k, 0)) * (u - up(u, 0)), 0.0)
        out = out + (flux - down(flux, 0))
        if flux_x is not None:
            out = out - flux_x
        r, k_now = extended(2, p, f_ref, zf_ref), k
        if p < NX - 1:
            un, kn = extended(0, p + 1, u_ref, zu_ref), extended(1, p + 1, k_ref, zk_ref)
            flux_x = (k + kn) * (u - un)
            out = out + flux_x
            u, k = un, kn
        r = r - out
        ro_ref[p] = r
        if p % 2 == 0:
            r_pair, k_pair = r, k_now
        else:
            rc_ref[p // 2] = restrict_plane(r_pair + r, tmp_ref.at[p - 1], even, 0.125)
            kc_ref[p // 2] = restrict_plane(k_pair + k_now, tmp_ref.at[p], even, 0.03125)


def edge_kernel(
    u_ref, k_ref, r_ref, rcl_ref, kcl_ref, zu_ref, zk_ref, zf_ref, one_ref, two_ref,
    uo_ref, ko_ref, k_in_ref, r_in_ref, rc_ref, kc_ref, chip_ref, link_ref,
    tmp_ref,
):
    core = lax.rem(lax.axis_index("pencil"), 2)
    row = lax.broadcasted_iota(jnp.int32, (H, ZE), 0)
    even = lanes((CY, ZE)) % 2 == 0

    pair = lax.broadcasted_iota(jnp.int32, (H, NZ), 0) // 2

    def tiles(g):
        one, two = one_ref[g], two_ref[g]
        return jnp.where(core == 1, one, two), jnp.where(core == 1, two, one)

    def halo(i, p, beyond):
        if i < 2 or p < NX - 2:
            after, before = tiles(i * NX + p)
        else:
            after = before = jnp.zeros((H, NZ), f32)
            for j in range(3):
                a, b = tiles(2 * NX + 3 * (p - NX + 2) + j)
                after = jnp.where(pair == j, pltpu.roll(a, 2 + 2 * j, 0), after)
                before = jnp.where(pair == j + 1, pltpu.roll(b, 2 + 2 * j, 0), before)
        cells = jnp.concatenate([after, before], axis=0)
        return jnp.concatenate([0.5 * cells if i == 1 else cells, beyond[p]], axis=1)

    flux_x = r_pair = k_pair = d_pair = None
    u, k = halo(0, 0, zu_ref), halo(1, 0, zk_ref)
    for p in range(NX):
        own_u, own_k, own_r = u_ref[p], k_ref[p], r_ref[p]
        flux = (k + up(k, 1)) * (u - up(u, 1))
        out = flux - down(flux, 1)
        kl, ul, kv, uv = k[:H], u[:H], k[H:], u[H:]
        low = (down(own_k[H:], 0) + kl) * (down(own_u[H:], 0) - ul)
        high = (kv + up(own_k[:H], 0)) * (uv - up(own_u[:H], 0))
        flux = (kl + up(kl, 0)) * (ul - up(ul, 0))
        below = flux - jnp.where(row == 0, low, down(flux, 0))
        flux = jnp.where(row == H - 1, high, (kv + up(kv, 0)) * (uv - up(uv, 0)))
        out = out + jnp.concatenate([below, flux - down(flux, 0)], axis=0)
        first = jnp.where(row == 0, down(high, 0), 0.0)
        last = jnp.where(row == H - 1, up(low, 0), 0.0)
        if flux_x is not None:
            out = out - flux_x
        r, k_now, u_now = halo(2, p, zf_ref), k, u
        if p < NX - 1:
            un, kn = halo(0, p + 1, zu_ref), halo(1, p + 1, zk_ref)
            flux_x = (k + kn) * (u - un)
            out = out + flux_x
            u, k = un, kn
        r = r - out
        q = place(core, p, NX)
        near = row < H // 2
        r_in_ref[q] = jnp.concatenate(
            [own_r[:H] + first, own_r[H:] - last, jnp.where(near, r[:H], r[H:])], axis=0
        )
        k_in_ref[q] = jnp.concatenate([own_k, jnp.where(near, k_now[:H], k_now[H:])], axis=0)
        if p in (0, NX - 1):
            end = place(core, p // (NX - 1), 2)
            uo_ref[end] = jnp.concatenate([own_u, u_now], axis=0)
            ko_ref[end] = jnp.concatenate([own_k, k_now], axis=0)
        if p % 2 == 0:
            r_pair, k_pair, d_pair = r, k_now, first - last
        else:
            c = place(core, p // 2, CX)
            rc_ref[c] = jnp.concatenate([
                rcl_ref[p // 2] + 0.125 * lane_pairs(d_pair + (first - last), even),
                restrict_plane(r_pair + r, tmp_ref.at[p - 1], even, 0.125),
            ], axis=0)
            kc_ref[c] = jnp.concatenate(
                [kcl_ref[p // 2], restrict_plane(k_pair + k_now, tmp_ref.at[p], even, 0.03125)], axis=0
            )
    even_c = lanes((CE, ZE)) % 2 == 0
    for i, ref in enumerate((link_ref, chip_ref)):
        at, step, c = i * (NX - 1), 1 - 2 * i, i * (CX - 1)
        tails = {}
        send_rows(ref, tails, X_U, uo_ref[i])
        send_rows(ref, tails, X_K, ko_ref[i])
        send_rows(ref, tails, X_K2, k_in_ref[at + step])
        send_rows(ref, tails, X_K3, k_in_ref[at + 2 * step, :NY])
        send_rows(ref, tails, X_R1, r_in_ref[at])
        send_rows(ref, tails, X_R2, r_in_ref[at + step, :NY])
        for d in range(CX):
            both = jnp.where(even_c, rc_ref[c + d * step], kc_ref[c + d * step])
            send_rows(ref, tails, X_C + 2 * d, both if d < 3 else both[:CY])
        send_tails(ref, tails)


def faces_yz(k, by=1):
    ky, kz = k + up(k, 0), k + up(k, 1, by)
    return ky, kz, (ky + down(ky, 0)) + (kz + down(kz, 1, by))


def flux_yz(v, ky, kz, by=1):
    flux = kz * (v - up(v, 1, by))
    out = flux - down(flux, 1, by)
    flux = ky * (v - up(v, 0))
    return out + (flux - down(flux, 0))


def inverse(k, diag, scale=1.0):
    return jnp.where(k > 0.0, scale / diag, 0.0)


def step_d1(r1, d0, inv):
    return (RHO1 * RHO0) * d0 + (2.0 * RHO1 / DELTA) * (r1 * inv)


def main(v):
    return v[:NY, :NZ]


def open_message(msg, u_end, k_end, r_end, rc_end, tmp_ref):
    even_c = lanes((CE, ZE)) % 2 == 0
    none = jnp.zeros((RF - NY, ZE), f32)
    un, kn = received_rows(msg, X_U, 4), received_rows(msg, X_K, 4)
    flux = (k_end + kn) * (u_end - un)
    inner = inner_rows(flux)
    coarse = restrict_plane(flux, tmp_ref, even_c, 0.125)
    ks = [inner_rows(kn), received_rows(msg, X_K2, 3)]
    ks.append(jnp.concatenate([received_rows(msg, X_K3, 2), none], axis=0))
    rs = [received_rows(msg, X_R1, 3) + inner]
    rs.append(jnp.concatenate([received_rows(msg, X_R2, 2), none], axis=0))
    kcs, rcs = [], []
    for d in range(CX):
        if d < 3:
            both = received_rows(msg, X_C + 2 * d, 2)
            rc = jnp.where(even_c, both, down(both, 1))
            rcs.append(rc + coarse if d == 0 else rc)
        else:
            both = jnp.concatenate([received_rows(msg, X_C + 2 * d, 1), none], axis=0)
        kcs.append(jnp.where(even_c, up(both, 1), both))
    return r_end - inner, ks, rs, rc_end - coarse, kcs, rcs


OFF, COFF = 3, 4


def at(near, own, s, first, inward, off=OFF):
    return own[inward(s)] if s >= first else near[off + s]


def fine_side(opened, inward, own, near, emit):
    r_end, ks, rs = opened[:3]
    k, r, ky, kz, inv, d0, r1, d1 = own
    k_x, r_x, ky_x, kz_x, inv_x, d0_x, d1_x = near
    for d, plane in enumerate(ks):
        k_x[OFF - 1 - d] = plane
    for d, plane in enumerate([r_end] + rs):
        r_x[OFF - d] = plane

    def k_at(s):
        return at(k_x, k, s, 0, inward)

    def d0_at(s):
        return at(d0_x, d0, s, 1, inward)

    def d1_at(s):
        return at(d1_x, d1, s, 2, inward)

    def faces_at(s):
        return at(ky_x, ky, s, 0, inward), at(kz_x, kz, s, 0, inward)

    kx = k_at(-3) + k_at(-2)
    for s in range(-2, 1):
        kv = k_at(s)
        before, kx = kx, kv + k_at(s + 1)
        if s < 0:
            ky_x[OFF + s], kz_x[OFF + s], diag = faces_yz(kv)
            diag = diag + before + kx
        else:
            diag = inv[inward(0)] + before
        scale = inverse(kv, diag)
        inv_x[OFF + s] = scale
        d0_x[OFF + s] = r_x[OFF + s] * scale * (1.0 / THETA)
    flux_x = (k_at(-2) + k_at(-1)) * (d0_at(-2) - d0_at(-1))
    for s in range(-1, 2):
        v = d0_at(s)
        out = flux_yz(v, *faces_at(s)) - flux_x
        flux_x = (k_at(s) + k_at(s + 1)) * (v - d0_at(s + 1))
        rv = at(r_x, r, s, 1, inward) - (out + flux_x)
        r_x[OFF + s] = rv
        d1_x[OFF + s] = step_d1(rv, v, at(inv_x, inv, s, 1, inward))
    flux_x = main((k_at(-1) + k_at(0)) * (d1_at(-1) - d1_at(0)))
    for s in range(3):
        v = d1_at(s)
        out = main(flux_yz(v, *faces_at(s))) - flux_x
        flux_x = main((k_at(s) + k_at(s + 1)) * (v - d1_at(s + 1)))
        rest = main(at(r_x, r1, s, 2, inward)) - (out + flux_x)
        emit(s, rest, main(d0_at(s)) + main(v) if s < 2 else None)


def coarse_side(opened, inward, kc, cinv, near):
    rc_end, kcs, rcs = opened[3:]
    q_x, s_x, cy_x, cz_x, cinv_x, e0_x = near
    for d, plane in enumerate(kcs):
        q_x[COFF - 1 - d] = plane
    for d, plane in enumerate([rc_end] + rcs):
        s_x[COFF - d] = plane
    kx = q_x[COFF - 4] + q_x[COFF - 3]
    for s in range(-3, 1):
        k = at(q_x, kc, s, 0, inward, COFF)
        before, kx = kx, k + at(q_x, kc, s + 1, 0, inward, COFF)
        if s < 0:
            cy_x[COFF + s], cz_x[COFF + s], diag = faces_yz(k, 2)
            diag = diag + before + kx
        else:
            diag = cinv[inward(0)] + before
        scale = inverse(k, diag, 0.8)
        cinv_x[COFF + s] = scale
        e0_x[COFF + s] = s_x[COFF + s] * scale


def sweep(first, last, e_at, q_at, rc_at, cy_at, cz_at, cinv_at, emit):
    flux_x = (q_at(first - 1) + q_at(first)) * (e_at(first - 1) - e_at(first))
    for c in range(first, last + 1):
        e = e_at(c)
        out = flux_yz(e, cy_at(c), cz_at(c), 2) - flux_x
        flux_x = (q_at(c) + q_at(c + 1)) * (e - e_at(c + 1))
        emit(c, e + cinv_at(c) * (rc_at(c) - (out + flux_x)))


def mid_kernel(
    u_ref, k_ref, r_ref, rc_ref, kc_ref,
    ky_ref, kz_ref, inv_ref, d0_ref, r1_ref, d1_ref, sum_ref, smooth_ref,
    cy_ref, cz_ref, cinv_ref, e0_ref,
):
    core = lax.rem(lax.axis_index("pencil"), 2)
    kx = None
    for p in range(NX):
        k = k_ref[p]
        ky_ref[p], kz_ref[p], diag = faces_yz(k)
        if kx is not None:
            diag = diag + kx
        if p < NX - 1:
            kx = k + k_ref[p + 1]
            diag = diag + kx
        if 0 < p < NX - 1:
            inv = inverse(k, diag)
            inv_ref[p] = inv
            d0_ref[p] = r_ref[p] * inv * (1.0 / THETA)
        else:
            inv_ref[p] = diag
    flux_x = (k_ref[1] + k_ref[2]) * (d0_ref[1] - d0_ref[2])
    for p in range(2, NX - 2):
        d0 = d0_ref[p]
        out = flux_yz(d0, ky_ref[p], kz_ref[p]) - flux_x
        flux_x = (k_ref[p] + k_ref[p + 1]) * (d0 - d0_ref[p + 1])
        r1 = r_ref[p] - (out + flux_x)
        d1 = step_d1(r1, d0, inv_ref[p])
        r1_ref[p], d1_ref[p] = r1, d1
        sum_ref[p] = u_ref[place(core, p, NX)] + main(d0) + main(d1)
    flux_x = main((k_ref[2] + k_ref[3]) * (d1_ref[2] - d1_ref[3]))
    for p in range(3, NX - 3):
        d1 = d1_ref[p]
        out = main(flux_yz(d1, ky_ref[p], kz_ref[p])) - flux_x
        flux_x = main((k_ref[p] + k_ref[p + 1]) * (d1 - d1_ref[p + 1]))
        smooth_ref[p] = main(r1_ref[p]) - (out + flux_x)
    kx = None
    for c in range(CX):
        k = kc_ref[c]
        cy_ref[c], cz_ref[c], diag = faces_yz(k, 2)
        if kx is not None:
            diag = diag + kx
        if c < CX - 1:
            kx = k + kc_ref[c + 1]
            diag = diag + kx
        if 0 < c < CX - 1:
            inv = inverse(k, diag, 0.8)
            cinv_ref[c] = inv
            e0_ref[c] = rc_ref[c] * inv
        else:
            cinv_ref[c] = diag


def chip_kernel(
    u_ref, uo_ref, ko_ref, k_ref, r_ref, rc_ref, kc_ref,
    ky_ref, kz_ref, inv_ref, d0_ref, r1_ref, d1_ref,
    cy_ref, cz_ref, cinv_ref, e0_ref, msg_ref,
    sum_ref, smooth_ref, q_x, s_x, cinv_x, e1_x, e2_x,
    k_x, r_x, ky_x, kz_x, inv_x, d0_x, d1_x, cy_x, cz_x, e0_x, tmp_ref,
):
    core = lax.rem(lax.axis_index("pencil"), 2)
    opened = open_message(msg_ref, uo_ref[1], ko_ref[1], r_ref[NX - 1], rc_ref[CX - 1], tmp_ref)

    def emit(s, rest, step):
        smooth_ref[s] = rest
        if s < 2:
            sum_ref[s] = u_ref[place(core, NX - 1 - s, NX)] + step

    fine_side(
        opened, lambda s: NX - 1 - s,
        (k_ref, r_ref, ky_ref, kz_ref, inv_ref, d0_ref, r1_ref, d1_ref),
        (k_x, r_x, ky_x, kz_x, inv_x, d0_x, d1_x), emit,
    )

    def inward(s):
        return CX - 1 - s

    coarse_side(opened, inward, kc_ref, cinv_ref, (q_x, s_x, cy_x, cz_x, cinv_x, e0_x))

    def pick(near, own, first):
        return lambda s: at(near, own, s, first, inward, COFF)

    rest = (
        pick(q_x, kc_ref, 0), pick(s_x, rc_ref, 1), pick(cy_x, cy_ref, 0), pick(cz_x, cz_ref, 0),
        pick(cinv_x, cinv_ref, 1),
    )

    def keep(ref):
        def store(s, e):
            ref[COFF + s] = e

        return store

    sweep(-2, 1, pick(e0_x, e0_ref, 1), *rest, keep(e1_x))
    sweep(-1, 0, lambda s: e1_x[COFF + s], *rest, keep(e2_x))


def final_kernel(
    u_ref, uo_ref, ko_ref, k_ref, r_ref, rc_ref, kc_ref,
    ky_ref, kz_ref, inv_ref, d0_ref, r1_ref, d1_ref, sum_ref, smooth_ref,
    cy_ref, cz_ref, cinv_ref, e0_ref,
    sum_c, smooth_c, q_c, s_c, cinv_c, e1_c, e2_c, msg_ref,
    new_hbm, smooth_hbm,
    k_x, r_x, ky_x, kz_x, inv_x, d0_x, d1_x, q_x, s_x, cy_x, cz_x, cinv_x, e0_x, e1_x, e2_x,
    tmp_ref, lift_ref, new_ref, out_ref, new_sem, smooth_sem,
):
    core = lax.rem(lax.axis_index("pencil"), 2)
    copies = []

    def put(src, dst, sem, p):
        copies.append(pltpu.make_async_copy(src, dst.at[place(core, p, NX)], sem.at[p]))
        copies[-1].start()

    for p in range(3, NX):
        put(smooth_ref.at[p] if p < NX - 3 else smooth_c.at[NX - 1 - p], smooth_hbm, smooth_sem, p)
    opened = open_message(msg_ref, uo_ref[0], ko_ref[0], r_ref[0], rc_ref[0], tmp_ref)

    def emit(p, rest, step):
        out_ref[p] = rest
        put(out_ref.at[p], smooth_hbm, smooth_sem, p)
        if p < 2:
            new_ref[p] = u_ref[place(core, p, NX)] + step

    fine_side(
        opened, lambda s: s,
        (k_ref, r_ref, ky_ref, kz_ref, inv_ref, d0_ref, r1_ref, d1_ref),
        (k_x, r_x, ky_x, kz_x, inv_x, d0_x, d1_x), emit,
    )
    coarse_side(opened, lambda s: s, kc_ref, cinv_ref, (q_x, s_x, cy_x, cz_x, cinv_x, e0_x))

    def pick(near, own, first, far=None, beyond=CX):
        def read(c):
            if c < first:
                return near[COFF + c]
            return own[c] if c < beyond else far[COFF + CX - 1 - c]

        return read

    rest = (
        pick(q_x, kc_ref, 0, q_c), pick(s_x, rc_ref, 1, s_c, 3), pick(cy_x, cy_ref, 0),
        pick(cz_x, cz_ref, 0), pick(cinv_x, cinv_ref, 1, cinv_c, 3),
    )

    def keep(ref):
        def store(c, e):
            ref[COFF + c] = e

        return store

    def lift(c, e):
        cols = []
        for t in range(NZ // 128):
            part = e[:CY, t * 128 : (t + 1) * 128]
            tile = lift_ref.at[2 * c + t]
            tile[pl.ds(0, CY, stride=2), :] = part
            tile[pl.ds(1, CY, stride=2), :] = part
            cols.append(tile[...])
        lifted = jnp.concatenate(cols, axis=1)
        for p in (2 * c, 2 * c + 1):
            if p < 2:
                done = new_ref[p]
            else:
                done = sum_ref[p] if p < NX - 2 else sum_c[NX - 1 - p]
            new_ref[p] = done + lifted
            put(new_ref.at[p], new_hbm, new_sem, p)

    sweep(-2, 1, pick(e0_x, e0_ref, 1), *rest, keep(e1_x))
    sweep(-1, 2, pick(e1_x, None, 2, e1_c, 2), *rest, keep(e2_x))
    sweep(0, 3, pick(e2_x, None, 3, e2_c, 3), *rest, lift)
    for copy in copies:
        copy.wait()


def call(kernel, outs, specs, scratch, bytes_accessed, flops):
    spaces = {"s": pltpu.SMEM, "v": pltpu.VMEM, "h": pltpu.HBM}
    return pl.pallas_call(
        kernel,
        out_shape=[jax.ShapeDtypeStruct(tuple(s), f32) for s in outs],
        in_specs=[pl.BlockSpec(memory_space=spaces[s]) for s in specs],
        out_specs=[
            pl.BlockSpec(memory_space=pl.ANY if isinstance(s, list) else pltpu.VMEM) for s in outs
        ],
        scratch_shapes=[pltpu.VMEM(s, f32) if isinstance(s, tuple) else s for s in scratch],
        compiler_params=pltpu.CompilerParams(vmem_limit_bytes=16 << 20),
        cost_estimate=pl.CostEstimate(flops=flops, bytes_accessed=bytes_accessed, transcendentals=0),
    )


def parted(cells, by):
    count = lax.axis_size("coarse")
    pairs = []
    for p in range(lax.axis_size("pencil")):
        step = by if p % 2 == 0 else -by
        pairs += [
            (p * count + i, p * count + i + step) for i in range(count) if 0 <= i + step < count
        ]
    return lax.ppermute(cells, ("pencil", "coarse"), pairs)


def swapped(cells, axis, first):
    count = lax.axis_size(axis)
    pairs = []
    for i in range(first, count - 1, 2):
        pairs += [(i, i + 1), (i + 1, i)]
    return lax.ppermute(cells, axis, pairs)


def on_device(right_side, conductivity, guess):
    own = (NX, NY, NZ)
    dma = pltpu.SemaphoreType.DMA
    u, k, f, one, two, ends = call(
        pack_kernel,
        [own, own, own, (GROUPS, H, NZ), (GROUPS, H, NZ), [16, 3, H, 128]],
        "hhh", [(2, 3, H, 128), dma((6,)), dma((6,))], 1 << 20, 1 << 18,
    )(*(pltpu.with_memory_space_constraint(a, pltpu.HBM) for a in (guess, conductivity, right_side)))
    one = parted(one, 1)
    two = parted(two, -1)
    ends = lax.all_to_all(ends, ("gz", "coarse"), 0, 0)

    def fine(n):
        return (n, RF, ZE)

    def coarse(n):
        return (n, CE, ZE)

    message = (X_GROUPS + 2, 8, NZ)
    edges = (ZE // 128, RE, 128)
    rows = [(NX, NY, ZE)] * 3 + [(CX, CY, ZE)] * 2
    tiles = [(NX, 2 * H, 128)] * 3
    parts = call(
        own_kernel, rows + tiles, "v" * 4, [(NX, ZE // 128, NY, 128)], 3 << 20, 1 << 22,
    )(u, k, f, ends)
    uo, ko, k_in, r_in, rc, kc, chip, link = call(
        edge_kernel,
        [(2, RE, ZE), (2, RE, ZE), fine(NX), fine(NX), coarse(CX), coarse(CX), message, message],
        "v" * 10, [(NX, ZE // 128, NY, 128)], 3 << 20, 1 << 22,
    )(*parts, one, two)
    chip = swapped(chip, "pencil", 0)
    link = swapped(link, "pencil", 1)
    *fine_own, sums, smooth, cy, cz, cinv, e0 = call(
        mid_kernel, [fine(NX)] * 6 + [own, own] + [coarse(CX)] * 4, "v" * 5, [],
        4 << 20, 1 << 22,
    )(u, k_in, r_in, rc, kc)
    half = call(
        chip_kernel,
        [(2, NY, NZ), (3, NY, NZ)] + [coarse(5)] * 3 + [coarse(6)] * 2, "v" * 18,
        [fine(3), fine(5)] + [fine(5)] * 5 + [coarse(5)] * 3 + [edges], 4 << 20, 1 << 22,
    )(u, uo, ko, k_in, r_in, rc, kc, *fine_own, cy, cz, cinv, e0, chip)
    return tuple(
        call(
            final_kernel, [list(own), list(own)], "v" * 27,
            [fine(3), fine(5)] + [fine(5)] * 5 + [coarse(5)] * 6 + [coarse(6), coarse(7)]
            + [edges, (NX, NY, 128), own, (3, NY, NZ), dma((NX,)), dma((NX,))],
            4 << 20, 1 << 22,
        )(u, uo, ko, k_in, r_in, rc, kc, *fine_own, sums, smooth, cy, cz, cinv, e0, *half, link)
    )


def solution(mesh):
    spec = P("pencil", "coarse", "gz")
    return jax.shard_map(
        on_device,
        mesh=mesh,
        in_specs=(spec, spec, spec),
        out_specs=(spec, spec),
        check_vma=False,
    )
```
